128 devices in a mesh: section: 8 (over y, core), hid: 16 (over z, x).
Axes of the slice: x: 4, y: 4, z: 4, core: 2. Of those that a mesh axis runs over, the one named last changes fastest.
Arguments:
- streams: float32 [8, 2, 512, 1024], P('section', None, 'hid'), may hold values from -6 to 6
- cotangents: float32 [8, 2, 512, 1024], P('section', None, 'hid'), may hold values from -0.6 to 0.6
- feed_streams: float32 [2, 2, 512, 1024], P(None, None, 'hid'), may hold values from -6 to 6
- feed_cotangents: float32 [2, 2, 512, 1024], P(None, None, 'hid'), may hold values from -0.6 to 0.6
- w_in: bfloat16 [8, 1024, 16384], P('section', None, 'hid'), may hold values from -0.1875 to 0.1875
- w_out: bfloat16 [8, 16384, 1024], P('section', 'hid'), may hold values from -0.046875 to 0.046875
- gain: float32 [8, 1024], P('section'), may hold values from 0.1 to 1.9
Outputs:
- out_streams: float32 [8, 2, 512, 1024], P('section', None, 'hid')
- out_cotangents: float32 [8, 2, 512, 1024], P('section', None, 'hid')
- grad_in: float32 [8, 1024, 16384], P('section', None, 'hid')
- grad_out: float32 [8, 16384, 1024], P('section', 'hid')
The draws below stay inside these ranges and needn't reach their ends.
All inputs are finite; a program needn't handle non-finite values.
Results may differ from the reference program's by a relative error of at most 0.0071.
Values may be sent and summed in bfloat16 or wider, within the bound.
A program may use at most 128 MiB of HBM per device.

```python
from functools import partial
import jax
import jax.numpy as jnp
from jax import lax

D = 1024
FF = 16384
ROWS = 512
TICKS = 3
SECTIONS = 8


def block_scale(rng, dims, shards, smallest, top_value):
    def one(axis_at, shards_of):
        draws = jax.random.uniform(jax.random.fold_in(jax.random.fold_in(rng, 6), axis_at), (shards_of,), jnp.float32, smallest / len(shards), top_value / len(shards))
        return jnp.repeat(jnp.exp(draws), dims[axis_at] // shards_of).reshape((-1,) + (1,) * (len(dims) - axis_at - 1))

    loudness = one(*shards[0])
    for cut in shards[1:]:
        loudness = loudness * one(*cut)
    return loudness


def centred(own_key, dims, deviation, limit, cuts=(), dtype=jnp.bfloat16):
    result = deviation * jax.random.normal(own_key, dims, jnp.float32)
    if cuts:
        result = result * block_scale(own_key, dims, cuts, -0.22, 0.18)
    return jnp.clip(result, -limit, limit).astype(dtype)


def setup_inputs(seed: int = 0) -> dict:
    streams_of = jax.random.split(jax.random.key(seed), 8)
    return {
        "streams": centred(streams_of[0], (SECTIONS, 2, ROWS, D), 1.0, 6.0, ((0, 8), (2, 16)), jnp.float32),
        "cotangents": centred(streams_of[1], (SECTIONS, 2, ROWS, D), 0.1, 0.6, ((0, 8), (2, 16)), jnp.float32),
        "feed_streams": centred(streams_of[2], (TICKS - 1, 2, ROWS, D), 1.0, 6.0, ((2, 16),), jnp.float32),
        "feed_cotangents": centred(streams_of[3], (TICKS - 1, 2, ROWS, D), 0.1, 0.6, ((2, 16),), jnp.float32),
        "w_in": centred(streams_of[4], (SECTIONS, D, FF), D ** -0.5, 0.1875, ((0, 8), (2, 16))),
        "w_out": centred(streams_of[5], (SECTIONS, FF, D), FF ** -0.5, 0.046875, ((0, 8), (1, 16))),
        "gain": jnp.clip(1.0 + 0.18 * jax.random.normal(streams_of[6], (SECTIONS, D), jnp.float32), 0.1, 1.9),
    }


def normalize(stream):
    mean_sq = lax.optimization_barrier(jnp.mean(stream * stream, axis=-1, keepdims=True))
    scale_row = lax.rsqrt(mean_sq + 1e-06)
    return (stream * scale_row, scale_row)

def back_step(first, second, grad_first, grad_second, weight_in, weight_out, gain_row):
    normed, scale_row = normalize(first)
    lifted = (normed * gain_row).astype(jnp.bfloat16)
    pre = jnp.dot(lifted, weight_in, preferred_element_type=jnp.float32)
    hidden = jax.nn.gelu(pre, approximate=True).astype(jnp.bfloat16)
    restored = second - jnp.dot(hidden, weight_out, preferred_element_type=jnp.float32)
    cotan = grad_second.astype(jnp.bfloat16)
    back_hidden = jnp.dot(cotan, weight_out.T, preferred_element_type=jnp.float32)
    unused, pull = jax.vjp(partial(jax.nn.gelu, approximate=True), pre)
    back_pre = pull(back_hidden)[0].astype(jnp.bfloat16)
    back_lift = jnp.dot(back_pre, weight_in.T, preferred_element_type=jnp.float32)
    back_norm = back_lift * gain_row
    grad_stream = grad_first + scale_row * (back_norm - normed * lax.optimization_barrier(jnp.mean(back_norm * normed, axis=-1, keepdims=True)))
    grad_win = jnp.dot(lifted.T, back_pre, preferred_element_type=jnp.float32)
    grad_wout = jnp.dot(hidden.T, cotan, preferred_element_type=jnp.float32)
    return (restored, grad_stream, grad_win, grad_wout)

def one_section(items):
    held, held_cot, weight_in, weight_out, gain_row = items
    restored, grad_stream, grad_win, grad_wout = back_step(held[0], held[1], held_cot[0], held_cot[1], weight_in, weight_out, gain_row)
    new_streams = jnp.stack([restored, held[0]])
    new_cot = jnp.stack([held_cot[1], grad_stream])
    return (new_streams, new_cot, grad_win, grad_wout)

def reference(streams, cotangents, feed_streams, feed_cotangents, w_in, w_out, gain):
    total_in = jnp.zeros(w_in.shape, jnp.float32)
    total_out = jnp.zeros(w_out.shape, jnp.float32)
    held, held_cot = (streams, cotangents)
    for tick_num in range(TICKS):
        new_streams, new_cot, grad_win, grad_wout = lax.map(one_section, (held, held_cot, w_in, w_out, gain))
        total_in = total_in + grad_win
        total_out = total_out + grad_wout
        if tick_num < TICKS - 1:
            held = jnp.concatenate([new_streams[1:], feed_streams[tick_num][None]], axis=0)
            held_cot = jnp.concatenate([new_cot[1:], feed_cotangents[tick_num][None]], axis=0)
    return (new_streams, new_cot, total_in, total_out)
```

```python
from functools import partial

import jax
import jax.numpy as jnp
from jax import lax
from jax.experimental import pallas as pl
from jax.experimental.pallas import tpu as pltpu
from jax.sharding import PartitionSpec as P

MESH = pl.DeviceIdType.MESH
BF = jnp.bfloat16
F32 = jnp.float32
CHUNKS = 2
SIDE = 4
TILE = 256
N_COPY = 48
GELU_A = 0.044715
GELU_C = 0.7978845608028654


def dot_nn(a, b):
    return lax.dot_general(a, b, (((1,), (0,)), ((), ())), preferred_element_type=F32)


def dot_nt(a, b):
    return lax.dot_general(a, b, (((1,), (1,)), ((), ())), preferred_element_type=F32)


def dot_tn(a, b):
    return lax.dot_general(a, b, (((0,), (0,)), ((), ())), preferred_element_type=F32)


def kernel(
    streams, cots, feed_s, feed_c, w_in_hbm, w_out_hbm, gain_hbm,
    out_s, out_c, out_gin, out_gout,
    st, ct, fs, fc, w_in, w_out, gain,
    held, got, shift,
    ga, gb, hid, bpre, pa, pb,
    big_f, big_d, big_e, big_c, summed, summed_b, small_f, small_d, small_e, small_c,
    acc_in, acc_out,
    ssem, rsem, lsem,
):
    ticks = feed_s.shape[0] + 1
    rows, width = st.shape[1], st.shape[2]
    r = rows // CHUNKS
    half = width // 2
    sections = lax.axis_size("section")
    sec = lax.axis_index("section")
    h = lax.axis_index("hid")
    x, z = lax.rem(h, SIDE), lax.div(h, SIDE)
    top = sec == sections - 1

    def wrap(v, by):
        return lax.rem(v + (by + SIDE), SIDE)

    def along_x(by):
        return {"hid": z * SIDE + wrap(x, by)}

    def along_z(by):
        return {"hid": wrap(z, by) * SIDE + x}

    below = {"section": lax.rem(sec + sections - 1, sections)}
    above = {"section": lax.rem(sec + 1, sections)}

    loads = []

    def load(i, src, dst):
        copy = pltpu.make_async_copy(src, dst, lsem.at[i])
        copy.start()
        return copy

    first_loads = [load(0, streams.at[0], st), load(1, cots.at[0], ct), load(2, gain_hbm, gain)]
    weight_loads = [load(3, w_in_hbm.at[0], w_in), load(4, w_out_hbm.at[0], w_out)]
    feed_loads = [load(5, feed_s, fs), load(6, feed_c, fc)]

    barrier = pltpu.get_barrier_semaphore()
    for peer in (along_x(1), along_x(-1), along_z(1), along_z(-1), above, below):
        pl.semaphore_signal(barrier, inc=1, device_id=peer, device_id_type=MESH)
    pl.semaphore_wait(barrier, 6)
    for copy in first_loads:
        copy.wait()

    class Lane:
        def __init__(self, q, which):
            self.q, self.which = q, which
            if which == 0:
                self.m, self.big = x, z
                self.small_dev, self.big_dev = along_x, along_z
                self.g, self.p = ga.at[q], pa.at[q]
            else:
                self.m, self.big = z, x
                self.small_dev, self.big_dev = along_z, along_x
                self.g, self.p = gb.at[q], pb.at[q]
            self.base = which * 22

        def single(self, ref, big, m):
            return ref.at[big, m] if self.which == 0 else ref.at[m, big]

        def pair(self, ref, big, part):
            two = pl.ds(2 * part, 2)
            return ref.at[big, two] if self.which == 0 else ref.at[two, big]

        def copy(self, i, src, dst, dev):
            return pltpu.make_async_remote_copy(
                src_ref=src, dst_ref=dst,
                send_sem=ssem.at[self.q, self.base + i], recv_sem=rsem.at[self.q, self.base + i],
                device_id=dev, device_id_type=MESH,
            )

        def send(self, i, src, dst, dev):
            self.copy(i, src, dst, dev).start()
            waits.append((self.q, self.base + i, src))

        def arrived(self, i, dst):
            self.copy(i, dst, dst, self.small_dev(1)).wait_recv()

        def a0(self):
            own = self.single(self.g, self.big, self.m)
            self.send(0, own, own, self.small_dev(1))
            self.send(1, own, own, self.small_dev(-1))

        def a1(self):
            lower = self.single(self.g, self.big, wrap(self.m, -1))
            upper = self.single(self.g, self.big, wrap(self.m, 1))
            self.arrived(0, lower)
            left = lower.at[:, pl.ds(0, half)]
            self.send(2, left, left, self.small_dev(1))
            self.arrived(1, upper)
            right = upper.at[:, pl.ds(half, half)]
            self.send(3, right, right, self.small_dev(-1))

        def a2(self):
            far = self.single(self.g, self.big, wrap(self.m, 2))
            self.arrived(2, far.at[:, pl.ds(0, half)])
            self.arrived(3, far.at[:, pl.ds(half, half)])
            one, two = self.pair(self.g, self.big, 0), self.pair(self.g, self.big, 1)
            self.send(4, one, one, self.big_dev(1))
            self.send(5, two, two, self.big_dev(-1))
            self.send(6, two, two, self.big_dev(1))
            self.send(7, one, one, self.big_dev(-1))

        def a3(self):
            one = self.pair(self.g, wrap(self.big, -1), 0)
            two = self.pair(self.g, wrap(self.big, 1), 1)
            self.arrived(4, one)
            self.send(8, one, one, self.big_dev(1))
            self.arrived(5, two)
            self.send(9, two, two, self.big_dev(-1))

        def a4(self):
            self.arrived(6, self.pair(self.g, wrap(self.big, -1), 1))
            self.arrived(7, self.pair(self.g, wrap(self.big, 1), 0))
            self.arrived(8, self.pair(self.g, wrap(self.big, 2), 0))
            self.arrived(9, self.pair(self.g, wrap(self.big, 2), 1))

        def slot(self, ref, i):
            return ref.at[self.q, self.which, i]

        def r0(self):
            p = self.p
            up, down, far = wrap(self.big, 1), wrap(self.big, -1), wrap(self.big, 2)
            self.send(10, self.pair(p, far, 0), self.slot(big_f, 0), self.big_dev(1))
            self.send(11, self.pair(p, far, 1), self.slot(big_f, 1), self.big_dev(-1))
            self.send(12, self.pair(p, up, 1), self.slot(big_d, 0), self.big_dev(1))
            self.send(13, self.pair(p, down, 0), self.slot(big_d, 1), self.big_dev(-1))

        def r1(self):
            for i, by in ((0, 1), (1, -1)):
                arrived, both = self.slot(big_f, i), self.slot(big_c, i)
                self.arrived(10 + i, arrived)
                own = self.pair(self.p, wrap(self.big, by), i)[...]
                both[...] = (own.astype(F32) + arrived[...].astype(F32)).astype(BF)
                self.send(14 + i, both, self.slot(big_e, i), self.big_dev(by))

        def r2(self):
            for i in (0, 1):
                self.arrived(12 + i, self.slot(big_d, i))
                self.arrived(14 + i, self.slot(big_e, i))
            total, total_b = summed.at[self.q % CHUNKS, self.which], summed_b.at[self.q, self.which]
            for part in (0, 1):
                value = (
                    self.pair(self.p, self.big, part)[...].astype(F32)
                    + self.slot(big_e, part)[...].astype(F32)
                    + self.slot(big_d, 1 - part)[...].astype(F32)
                )
                total[pl.ds(2 * part, 2)] = value
                total_b[pl.ds(2 * part, 2)] = value.astype(BF)
            up, down, far = wrap(self.m, 1), wrap(self.m, -1), wrap(self.m, 2)
            left, right = pl.ds(0, half), pl.ds(half, half)
            self.send(16, total_b.at[far, :, left], self.slot(small_f, 0), self.small_dev(1))
            self.send(17, total_b.at[far, :, right], self.slot(small_f, 1), self.small_dev(-1))
            self.send(18, total_b.at[up, :, right], self.slot(small_d, 0), self.small_dev(1))
            self.send(19, total_b.at[down, :, left], self.slot(small_d, 1), self.small_dev(-1))

        def r3(self):
            total = summed.at[self.q % CHUNKS, self.which]
            for i, by in ((0, 1), (1, -1)):
                arrived, both = self.slot(small_f, i), self.slot(small_c, i)
                self.arrived(16 + i, arrived)
                own = total[wrap(self.m, by), :, pl.ds(i * half, half)]
                both[...] = (own + arrived[...].astype(F32)).astype(BF)
                self.send(20 + i, both, self.slot(small_e, i), self.small_dev(by))

        def r4(self):
            total = summed.at[self.q % CHUNKS, self.which]
            for i in (0, 1):
                self.arrived(18 + i, self.slot(small_d, i))
                self.arrived(20 + i, self.slot(small_e, i))
            parts = [
                total[self.m, :, pl.ds(i * half, half)]
                + self.slot(small_e, i)[...].astype(F32)
                + self.slot(small_d, 1 - i)[...].astype(F32)
                for i in (0, 1)
            ]
            return jnp.concatenate(parts, axis=-1)

    waits = []
    out_copies = []

    def pass_on(q, i, src, dst):
        copy = pltpu.make_async_remote_copy(
            src_ref=src, dst_ref=dst, send_sem=ssem.at[q, 44 + i], recv_sem=rsem.at[q, 44 + i],
            device_id=below, device_id_type=MESH,
        )
        copy.start()
        waits.append((q, 44 + i, src))

    def normalized(first):
        scale_row = lax.rsqrt(jnp.mean(first * first, axis=-1, keepdims=True) + 1e-06)
        return first * scale_row, scale_row

    class Chunk:
        def __init__(self, t, c):
            self.t, self.c, self.q = t, c, t * CHUNKS + c
            self.rows = pl.ds(c * r, r)
            self.lanes = (Lane(self.q, 0), Lane(self.q, 1))

        def start(self):
            t, q = self.t, self.q
            mine = held.at[q]
            if t == 0:
                mine[0], mine[1] = st[0, self.rows], st[1, self.rows]
                mine[2], mine[3] = ct[0, self.rows], ct[1, self.rows]
            else:
                before = q - CHUNKS
                came = got.at[before]
                for i, place in ((0, 1), (1, 2), (2, 0), (3, 3)):
                    pltpu.make_async_remote_copy(
                        src_ref=came.at[place], dst_ref=came.at[place],
                        send_sem=ssem.at[before, 44 + i], recv_sem=rsem.at[before, 44 + i],
                        device_id=below, device_id_type=MESH,
                    ).wait_recv()
                for i, (feed, part) in enumerate(((fs, 0), (fs, 1), (fc, 0), (fc, 1))):
                    mine[i] = jnp.where(top, feed[t - 1, part, self.rows], came[i])
            normed, _ = normalized(mine[0])
            ga[q, z, x] = (normed * gain[...]).astype(BF)
            gb[q, z, x] = mine[3].astype(BF)
            for lane in self.lanes:
                lane.a0()
            if t < ticks - 1:
                pass_on(q, 0, mine.at[0], got.at[q, 1])
                pass_on(q, 1, mine.at[3], got.at[q, 2])

        def step(self, name):
            for lane in self.lanes:
                getattr(lane, name)()

        def k1(self):
            q = self.q
            n = SIDE * SIDE * r

            def body(j, carry):
                cols = pl.ds(pl.multiple_of(j * TILE, TILE), TILE)
                pre = dot_nn(ga[q].reshape(n, width), w_in[:, cols])
                back = dot_nt(gb[q].reshape(n, width), w_out[cols, :])
                sq = pre * pre
                th = jnp.tanh(pre * (GELU_C + (GELU_C * GELU_A) * sq))
                cdf = 0.5 + 0.5 * th
                slope = cdf + (0.5 * pre) * (1.0 - th * th) * (GELU_C + (3.0 * GELU_C * GELU_A) * sq)
                hid[q, :, cols] = (pre * cdf).astype(BF)
                bpre[q, :, cols] = (back * slope).astype(BF)
                return carry

            lax.fori_loop(0, w_in.shape[1] // TILE, body, 0)

        def k2(self):
            q = self.q

            def body(j, carry):
                cols = pl.ds(pl.multiple_of(j * TILE, TILE), TILE)
                out = dot_nn(hid[q], w_out[:, cols])
                pa[q, :, :, :, cols] = out.astype(BF).reshape(SIDE, SIDE, r, TILE)
                lift = dot_nt(bpre[q], w_in[cols, :])
                pb[q, :, :, :, cols] = lift.astype(BF).reshape(SIDE, SIDE, r, TILE)
                return carry

            lax.fori_loop(0, width // TILE, body, 0)

        def finish(self):
            t, q = self.t, self.q
            mine = held.at[q]
            block_out = self.lanes[0].r4()
            back_lift = self.lanes[1].r4()
            normed, scale_row = normalized(mine[0])
            back_norm = back_lift * gain[...]
            shift[q, 0] = mine[1] - block_out
            shift[q, 1] = mine[2] + scale_row * (
                back_norm - normed * jnp.mean(back_norm * normed, axis=-1, keepdims=True)
            )
            if t < ticks - 1:
                pass_on(q, 2, shift.at[q, 0], got.at[q, 0])
                pass_on(q, 3, shift.at[q, 1], got.at[q, 3])
            else:
                for i, (src, dst, part) in enumerate((
                    (shift.at[q, 0], out_s, 0), (mine.at[0], out_s, 1),
                    (mine.at[3], out_c, 0), (shift.at[q, 1], out_c, 1),
                )):
                    out_copies.append(load(7 + 4 * self.c + i, src, dst.at[0, part, self.rows]))

    pieces = []

    def weight_piece(t, which, lo, count):
        left, right, acc, out = (
            (ga, bpre, acc_in, out_gin) if which == 0 else (hid, gb, acc_out, out_gout)
        )
        n = SIDE * SIDE * r

        def whole(ref, cols):
            if ref is ga or ref is gb:
                parts = [ref[t * CHUNKS + c, :, :, :, cols].reshape(n, -1) for c in range(CHUNKS)]
            else:
                parts = [ref[t * CHUNKS + c, :, cols] for c in range(CHUNKS)]
            return jnp.concatenate(parts, axis=0)

        def body(j, carry):
            cols = pl.ds(pl.multiple_of(j * TILE, TILE), TILE)
            part = dot_tn(whole(left, cols), whole(right, pl.ds(0, width)))
            acc[cols, :] = part if t == 0 else acc[cols, :] + part
            return carry

        lax.fori_loop(lo, lo + count, body, 0)
        if t == ticks - 1:
            span = pl.ds(lo * TILE, count * TILE)
            out_copies.append(load(16 + 4 * which + lo, acc.at[span], out.at[0, span]))

    def fill(count):
        for _ in range(count):
            if pieces:
                weight_piece(*pieces.pop(0))

    def ready(t):
        for which in (0, 1):
            for lo in (0, 2):
                pieces.append((t, which, lo, 2))

    prev = None
    for t in range(ticks):
        c0, c1 = Chunk(t, 0), Chunk(t, 1)
        c0.start()
        if prev:
            prev.step("r1")
        c0.step("a1")
        if prev:
            prev.step("r2")
        c0.step("a2")
        if prev:
            prev.step("r3")
            fill(1)
        c0.step("a3")
        if prev:
            prev.finish()
            fill(1)
        if t == 0:
            for copy in weight_loads + feed_loads:
                copy.wait()
        if not prev:
            c1.start()
        c0.step("a4")
        if not prev:
            c1.step("a1")
        c0.k1()
        if prev:
            c1.start()
        else:
            c1.step("a2")
        c0.k2()
        c0.step("r0")
        if prev:
            c1.step("a1")
            c1.step("a2")
        c0.step("r1")
        c1.step("a3")
        c0.step("r2")
        c1.step("a4")
        c0.step("r3")
        c1.k1()
        c0.finish()
        c1.k2()
        c1.step("r0")
        ready(t)
        fill(2)
        prev = c1
    prev.step("r1")
    fill(1)
    prev.step("r2")
    fill(1)
    prev.step("r3")
    fill(2)
    prev.finish()
    fill(len(pieces))
    for copy in out_copies:
        copy.wait()
    for q, i, src in waits:
        pltpu.make_async_remote_copy(
            src_ref=src, dst_ref=src, send_sem=ssem.at[q, i], recv_sem=rsem.at[q, i],
            device_id=below, device_id_type=MESH,
        ).wait_send()


def shards(streams, cotangents, feed_streams, feed_cotangents, w_in, w_out, gain):
    ticks = feed_streams.shape[0] + 1
    rows, width = streams.shape[2], streams.shape[3]
    hidden = w_in.shape[2]
    r = rows // CHUNKS
    n = SIDE * SIDE * r
    q = ticks * CHUNKS
    blocks = (q, SIDE, SIDE, r, width)
    hbm = pl.BlockSpec(memory_space=pl.ANY)
    half = width // 2
    return pl.pallas_call(
        kernel,
        out_shape=(
            jax.ShapeDtypeStruct(streams.shape, F32),
            jax.ShapeDtypeStruct(cotangents.shape, F32),
            jax.ShapeDtypeStruct(w_in.shape, F32),
            jax.ShapeDtypeStruct(w_out.shape, F32),
        ),
        in_specs=[hbm] * 7,
        out_specs=(hbm,) * 4,
        scratch_shapes=[
            pltpu.VMEM((2, rows, width), F32),
            pltpu.VMEM((2, rows, width), F32),
            pltpu.VMEM(feed_streams.shape, F32),
            pltpu.VMEM(feed_cotangents.shape, F32),
            pltpu.VMEM((width, hidden), BF),
            pltpu.VMEM((hidden, width), BF),
            pltpu.VMEM((1, width), F32),
            pltpu.VMEM((q, 4, r, width), F32),
            pltpu.VMEM((q - CHUNKS, 4, r, width), F32),
            pltpu.VMEM((q, 2, r, width), F32),
            pltpu.VMEM(blocks, BF),
            pltpu.VMEM(blocks, BF),
            pltpu.VMEM((q, n, hidden), BF),
            pltpu.VMEM((q, n, hidden), BF),
            pltpu.VMEM(blocks, BF),
            pltpu.VMEM(blocks, BF),
            pltpu.VMEM((q, 2, 2, 2, r, width), BF),
            pltpu.VMEM((q, 2, 2, 2, r, width), BF),
            pltpu.VMEM((q, 2, 2, 2, r, width), BF),
            pltpu.VMEM((q, 2, 2, 2, r, width), BF),
            pltpu.VMEM((CHUNKS, 2, SIDE, r, width), F32),
            pltpu.VMEM((q, 2, SIDE, r, width), BF),
            pltpu.VMEM((q, 2, 2, r, half), BF),
            pltpu.VMEM((q, 2, 2, r, half), BF),
            pltpu.VMEM((q, 2, 2, r, half), BF),
            pltpu.VMEM((q, 2, 2, r, half), BF),
            pltpu.VMEM((width, hidden), F32),
            pltpu.VMEM((hidden, width), F32),
            pltpu.SemaphoreType.DMA((q, N_COPY)),
            pltpu.SemaphoreType.DMA((q, N_COPY)),
            pltpu.SemaphoreType.DMA((24,)),
        ],
        compiler_params=pltpu.CompilerParams(
            collective_id=0, has_side_effects=True, vmem_limit_bytes=60 * 1024 * 1024
        ),
    )(streams, cotangents, feed_streams, feed_cotangents, w_in, w_out, gain)


def solution(mesh):
    placed = (
        P("section", None, "hid", None),
        P("section", None, "hid", None),
        P(None, None, "hid", None),
        P(None, None, "hid", None),
        P("section", None, "hid"),
        P("section", "hid", None),
        P("section", None),
    )
    return jax.shard_map(
        shards,
        mesh=mesh,
        in_specs=placed,
        out_specs=(
            P("section", None, "hid", None),
            P("section", None, "hid", None),
            P("section", None, "hid"),
            P("section", "hid", None),
        ),
        check_vma=False,
    )
```

```python
from functools import partial

import jax
import jax.numpy as jnp
from jax import lax
from jax.experimental import pallas as pl
from jax.experimental.pallas import tpu as pltpu
from jax.sharding import PartitionSpec as P

MESH = pl.DeviceIdType.MESH
BF = jnp.bfloat16
F32 = jnp.float32
CHUNKS = 2
SIDE = 4
TILE = 1024
GRAD_TILE = 256
STEPS = (2, 1, -1)
LANE_COPIES = 19
RELAY_GATHER = False
RELAY_SUM = False
PASS = 2 * LANE_COPIES
N_COPY = PASS + 3
GELU_A = 0.044715
GELU_C = 0.7978845608028654


def dot_nn(a, b):
    return lax.dot_general(a, b, (((1,), (0,)), ((), ())), preferred_element_type=F32)


def dot_nt(a, b):
    return lax.dot_general(a, b, (((1,), (1,)), ((), ())), preferred_element_type=F32)


def dot_tn(a, b):
    return lax.dot_general(a, b, (((0,), (0,)), ((), ())), preferred_element_type=F32)


ORDER = (
    (0, 0, 0, "S"), (0, 0, 1, "S"), (0, 1, 0, "S"), (0, 1, 1, "S"), (0, 0, 0, "a2"), (0, 0, 1, "a2"),
    (0, 1, 0, "a2"), (0, 1, 1, "a2"), (0, 0, 0, "a4"), (0, 0, 0, "K1"), (0, 0, 0, "K2"), (0, 0, 0, "r0"),
    (0, 0, 1, "a4"), (0, 0, 1, "K1"), (0, 0, 1, "K2"), (0, 0, 1, "r0"), (0, 1, 0, "a4"), (0, 1, 0, "K1"),
    (0, 1, 0, "K2"), (0, 1, 0, "r0"), (0, 1, 1, "a4"), (0, 1, 1, "K1"), (0, 1, 1, "K2"), (0, 1, 1, "r0"),
    (0, 0, 0, "r2"), (0, 0, 0, "W"), (0, 0, 2, "W"), (0, 0, 1, "r2"), (0, 1, 0, "W"), (0, 1, 2, "W"),
    (0, 1, 0, "r2"), (0, 1, 1, "r2"), (1, 0, 0, "S"), (1, 0, 1, "S"), (1, 1, 0, "S"), (1, 1, 1, "S"),
    (1, 0, 0, "a2"), (1, 0, 1, "a2"), (1, 1, 0, "a2"), (1, 1, 1, "a2"), (1, 0, 0, "a4"), (1, 0, 0, "K1"),
    (1, 0, 0, "K2"), (1, 0, 0, "r0"), (1, 0, 1, "a4"), (1, 0, 1, "K1"), (1, 0, 1, "K2"), (1, 0, 1, "r0"),
    (1, 1, 0, "a4"), (1, 1, 0, "K1"), (1, 1, 0, "K2"), (1, 1, 0, "r0"), (1, 1, 1, "a4"), (1, 1, 1, "K1"),
    (1, 1, 1, "K2"), (1, 1, 1, "r0"), (1, 0, 0, "r2"), (1, 0, 0, "W"), (1, 0, 2, "W"), (1, 0, 1, "r2"),
    (1, 1, 0, "W"), (1, 1, 2, "W"), (1, 1, 0, "r2"), (1, 1, 1, "r2"), (2, 0, 0, "S"), (2, 0, 1, "S"),
    (2, 1, 0, "S"), (2, 1, 1, "S"), (2, 0, 0, "a2"), (2, 0, 1, "a2"), (2, 1, 0, "a2"), (2, 1, 1, "a2"),
    (2, 0, 0, "a4"), (2, 0, 0, "K1"), (2, 0, 0, "K2"), (2, 0, 0, "r0"), (2, 0, 1, "a4"), (2, 0, 1, "K1"),
    (2, 0, 1, "K2"), (2, 0, 1, "r0"), (2, 1, 0, "a4"), (2, 1, 0, "K1"), (2, 1, 0, "K2"), (2, 1, 0, "r0"),
    (2, 1, 1, "a4"), (2, 1, 1, "K1"), (2, 1, 1, "K2"), (2, 1, 1, "r0"), (2, 0, 0, "r2"), (2, 0, 0, "W"),
    (2, 0, 2, "W"), (2, 0, 1, "r2"), (2, 1, 0, "W"), (2, 1, 2, "W"), (2, 1, 0, "r2"), (2, 0, 1, "F"),
    (2, 1, 1, "r2"), (2, 0, 0, "F"), (2, 1, 0, "F"), (2, 1, 1, "F"),
)


def order(ticks):
    return ORDER


def kernel(
    streams, cots, feed_s, feed_c, w_in_hbm, w_out_hbm, gain_hbm,
    out_s, out_c, out_gin, out_gout,
    st, ct, fs, fc, w_in, w_out, gain, gain_above,
    held, got, ga, gb, hid, bpre, pa, pb,
    big_r, slope, summed, summed_b, small_r,
    ssem, rsem, lsem,
):
    ticks = feed_s.shape[0] + 1
    rows, width = st.shape[1], st.shape[2]
    r = rows // CHUNKS
    n = SIDE * SIDE * r
    sections = lax.axis_size("section")
    sec = lax.axis_index("section")
    h = lax.axis_index("hid")
    x, z = lax.rem(h, SIDE), lax.div(h, SIDE)
    top = sec == sections - 1
    below = lax.rem(sec + sections - 1, sections)
    above = lax.rem(sec + 1, sections)

    def wrap(v, by):
        return lax.rem(v + (by + SIDE), SIDE)

    def along_x(by, section=sec):
        return {"section": section, "hid": z * SIDE + wrap(x, by)}

    def along_z(by, section=sec):
        return {"section": section, "hid": wrap(z, by) * SIDE + x}

    def load(i, src, dst):
        copy = pltpu.make_async_copy(src, dst, lsem.at[i])
        copy.start()
        return copy

    first_loads = [load(0, streams.at[0], st), load(1, cots.at[0], ct), load(2, gain_hbm, gain)]
    weight_loads = [load(3, w_in_hbm.at[0], w_in), load(4, w_out_hbm.at[0], w_out)]
    feed_loads = [load(5, feed_s, fs), load(6, feed_c, fc)]

    barrier = pltpu.get_barrier_semaphore()
    peers = [axis(by, s) for s in (sec, above, below) for axis in (along_x, along_z) for by in STEPS]
    peers += [along_x(0, above), along_x(0, below)]
    for peer in peers:
        pl.semaphore_signal(barrier, inc=1, device_id=peer, device_id_type=MESH)
    pl.semaphore_wait(barrier, len(peers))
    for copy in first_loads:
        copy.wait()

    waits = []

    def remote(q, i, src, dst, dev):
        return pltpu.make_async_remote_copy(
            src_ref=src, dst_ref=dst, send_sem=ssem.at[q, i], recv_sem=rsem.at[q, i],
            device_id=dev, device_id_type=MESH,
        )

    def send(q, i, src, dst, dev):
        remote(q, i, src, dst, dev).start()
        waits.append((q, i, src))

    def arrived(q, i, dst):
        remote(q, i, dst, dst, along_x(0, below)).wait_recv()

    class Lane:
        def __init__(self, t, q, which):
            self.t, self.q, self.which = t, q, which
            if which == 0:
                self.m, self.big = x, z
                self.small_dev, self.big_dev = along_x, along_z
                self.g, self.p = ga.at[q], pa.at[q]
            else:
                self.m, self.big = z, x
                self.small_dev, self.big_dev = along_z, along_x
                self.g, self.p = gb.at[q], pb.at[q]
            self.base = which * LANE_COPIES

        def single(self, ref, big, m):
            return ref.at[big, m] if self.which == 0 else ref.at[m, big]

        def group(self, ref, big):
            return ref.at[big] if self.which == 0 else ref.at[:, big]

        def pair(self, ref, big, part):
            two = pl.ds(2 * part, 2)
            return ref.at[big, two] if self.which == 0 else ref.at[two, big]

        def send(self, i, src, dst, dev):
            send(self.q, self.base + i, src, dst, dev)

        def arrived(self, i, dst):
            arrived(self.q, self.base + i, dst)

        def a0(self):
            own = self.single(self.g, self.big, self.m)
            for i, by in enumerate(STEPS):
                self.send(i, own, own, self.small_dev(by))

        def a2(self):
            for i, by in enumerate(STEPS):
                self.arrived(i, self.single(self.g, self.big, wrap(self.m, -by)))
            if RELAY_GATHER:
                one, two = self.pair(self.g, self.big, 0), self.pair(self.g, self.big, 1)
                self.send(3, one, one, self.big_dev(1))
                self.send(4, two, two, self.big_dev(-1))
                self.send(5, two, two, self.big_dev(1))
                self.send(6, one, one, self.big_dev(-1))
            else:
                mine = self.group(self.g, self.big)
                for i, by in enumerate(STEPS):
                    self.send(3 + i, mine, mine, self.big_dev(by))

        def a3(self):
            if RELAY_GATHER:
                one = self.pair(self.g, wrap(self.big, -1), 0)
                two = self.pair(self.g, wrap(self.big, 1), 1)
                self.arrived(3, one)
                self.send(7, one, one, self.big_dev(1))
                self.arrived(4, two)
                self.send(8, two, two, self.big_dev(-1))

        def a4(self):
            if RELAY_GATHER:
                self.arrived(5, self.pair(self.g, wrap(self.big, -1), 1))
                self.arrived(6, self.pair(self.g, wrap(self.big, 1), 0))
                self.arrived(7, self.pair(self.g, wrap(self.big, 2), 0))
                self.arrived(8, self.pair(self.g, wrap(self.big, 2), 1))
            else:
                for i, by in enumerate(STEPS):
                    self.arrived(3 + i, self.group(self.g, wrap(self.big, -by)))

        def slot(self, kind, i):
            return big_p.at[self.q, self.which, 2 * kind + i]

        def r0(self):
            if RELAY_SUM:
                up, down, far = wrap(self.big, 1), wrap(self.big, -1), wrap(self.big, 2)
                self.send(9, self.pair(self.p, far, 0), self.slot(0, 0), self.big_dev(1))
                self.send(10, self.pair(self.p, far, 1), self.slot(0, 1), self.big_dev(-1))
                self.send(11, self.pair(self.p, up, 1), self.slot(1, 0), self.big_dev(1))
                self.send(12, self.pair(self.p, down, 0), self.slot(1, 1), self.big_dev(-1))
            else:
                for i, by in enumerate(STEPS):
                    self.send(
                        9 + i, self.group(self.p, wrap(self.big, by)),
                        big_r.at[self.q, self.which, i], self.big_dev(by),
                    )

        def r1(self):
            if RELAY_SUM:
                for i, by in ((0, 1), (1, -1)):
                    came, both = self.slot(0, i), self.slot(3, i)
                    self.arrived(9 + i, came)
                    own = self.pair(self.p, wrap(self.big, by), i)[...]
                    both[...] = (own.astype(F32) + came[...].astype(F32)).astype(BF)
                    self.send(13 + i, both, self.slot(2, i), self.big_dev(by))

        def r2(self):
            last = self.t == ticks - 1
            total = summed_b.at[self.q, self.which]
            keep = summed.at[self.q % CHUNKS, self.which]
            if RELAY_SUM:
                for i in (0, 1):
                    self.arrived(11 + i, self.slot(1, i))
                    self.arrived(13 + i, self.slot(2, i))
                for part in (0, 1):
                    value = (
                        self.pair(self.p, self.big, part)[...].astype(F32)
                        + self.slot(2, part)[...].astype(F32)
                        + self.slot(1, 1 - part)[...].astype(F32)
                    )
                    if last:
                        keep[pl.ds(2 * part, 2)] = value
                    total[pl.ds(2 * part, 2)] = value.astype(BF)
            else:
                value = self.group(self.p, self.big)[...].astype(F32)
                for i in range(3):
                    self.arrived(9 + i, big_r.at[self.q, self.which, i])
                    value = value + big_r[self.q, self.which, i].astype(F32)
                if last:
                    keep[...] = value
                total[...] = value.astype(BF)
            for i, by in enumerate(STEPS if last else STEPS + (0,)):
                self.send(
                    15 + i, total.at[wrap(self.m, by)],
                    small_r.at[self.q, self.which, i], self.small_dev(by, sec if last else below),
                )

        def total(self):
            last = self.t == ticks - 1
            count = 3 if last else 4
            for i in range(count):
                self.arrived(15 + i, small_r.at[self.q, self.which, i])
            parts = [small_r[self.q, self.which, i].astype(F32) for i in range(count)]
            if last:
                parts.append(summed[self.q % CHUNKS, self.which, self.m])
            return (parts[0] + parts[1]) + (parts[2] + parts[3])

    def normalized(first):
        scale_row = lax.rsqrt(jnp.mean(first * first, axis=-1, keepdims=True) + 1e-06)
        return first * scale_row, scale_row

    def grad_of(first, grad_first, back_lift, gain_row):
        normed, scale_row = normalized(first)
        back_norm = back_lift * gain_row
        back = back_norm - normed * jnp.mean(back_norm * normed, axis=-1, keepdims=True)
        return grad_first + scale_row * back

    class Chunk:
        def __init__(self, t, c, before):
            self.t, self.c, self.q, self.before = t, c, t * CHUNKS + c, before
            self.rows = pl.ds(c * r, r)
            self.lanes = (Lane(t, self.q, 0), Lane(t, self.q, 1))

        def start(self, which):
            t, q = self.t, self.q
            mine = held.at[q]
            two = pl.ds(2 * which, 2)
            if t == 0:
                mine[two] = (ct if which else st)[:, self.rows]
            else:
                last_q = self.before.q
                came = got.at[last_q]
                arrived(last_q, PASS + which, came.at[two])
                total = self.before.lanes[which].total()
                if which == 0:
                    values = (came[1] - total, came[0])
                else:
                    values = (came[3], grad_of(came[0], came[2], total, gain_above[...]))
                feed = fc if which else fs
                for i in (0, 1):
                    mine[2 * which + i] = jnp.where(top, feed[t - 1, i, self.rows], values[i])
            if which == 0:
                ga[q, z, x] = (normalized(mine[0])[0] * gain[...]).astype(BF)
            else:
                gb[q, z, x] = mine[3].astype(BF)
            self.lanes[which].a0()
            if t < ticks - 1:
                send(q, PASS + which, mine.at[two], got.at[q, two], along_x(0, below))

        def finish(self, which):
            mine = held.at[self.q]
            total = self.lanes[which].total()
            if which == 0:
                out_s[0, 0, self.rows], out_s[0, 1, self.rows] = mine[1] - total, mine[0]
            else:
                out_c[0, 0, self.rows] = mine[3]
                out_c[0, 1, self.rows] = grad_of(mine[0], mine[2], total, gain[...])

        def tiles(self, body, size):
            def step(j, carry):
                body(pl.ds(pl.multiple_of(j * TILE, TILE), TILE))
                return carry

            lax.fori_loop(0, size // TILE, step, 0)

        def k1(self, which):
            q, c = self.q, self.c

            def lifted(cols):
                pre = dot_nn(ga[q].reshape(n, width), w_in[:, cols])
                sq = pre * pre
                th = jnp.tanh(pre * (GELU_C + (GELU_C * GELU_A) * sq))
                cdf = 0.5 + 0.5 * th
                hid[q, :, cols] = (pre * cdf).astype(BF)
                slope[c, :, cols] = cdf + (0.5 * pre) * (1.0 - th * th) * (
                    GELU_C + (3.0 * GELU_C * GELU_A) * sq
                )

            def cotan(cols):
                back = dot_nt(gb[q].reshape(n, width), w_out[cols, :])
                bpre[q, :, cols] = (back * slope[c, :, cols]).astype(BF)

            self.tiles(cotan if which else lifted, w_in.shape[1])

        def k2(self, which):
            q = self.q

            def block_out(cols):
                out = dot_nn(hid[q], w_out[:, cols])
                pa[q, :, :, :, cols] = out.astype(BF).reshape(SIDE, SIDE, r, TILE)

            def back_lift(cols):
                out = dot_nt(bpre[q], w_in[cols, :])
                pb[q, :, :, :, cols] = out.astype(BF).reshape(SIDE, SIDE, r, TILE)

            self.tiles(back_lift if which else block_out, width)

    def weight_piece(t, which, lo, count):
        left, right, acc = (ga, bpre, out_gin) if which == 0 else (hid, gb, out_gout)

        def whole(ref, cols):
            if ref is ga or ref is gb:
                parts = [ref[t * CHUNKS + c, :, :, :, cols].reshape(n, -1) for c in range(CHUNKS)]
            else:
                parts = [ref[t * CHUNKS + c, :, cols] for c in range(CHUNKS)]
            return jnp.concatenate(parts, axis=0)

        def body(j, carry):
            cols = pl.ds(pl.multiple_of(j * GRAD_TILE, GRAD_TILE), GRAD_TILE)
            part = dot_tn(whole(left, cols), whole(right, pl.ds(0, width)))
            acc[0, cols, :] = part if t == 0 else acc[0, cols, :] + part
            return carry

        lax.fori_loop(lo, lo + count, body, 0)

    chunks = {}
    for t in range(ticks):
        for c in range(CHUNKS):
            chunks[t, c] = Chunk(t, c, chunks.get((t - 1, c)))
    pending = {}

    def once(key, run):
        if key not in pending:
            pending[key] = True
            run()

    def wait_all(copies):
        for copy in copies:
            copy.wait()

    for t, c, which, what in order(ticks):
        if what == "W":
            weight_piece(t, c, which, 2)
            continue
        chunk = chunks[t, c]
        if what == "S":
            if t > 0:
                once("feed", lambda: wait_all(feed_loads))
                if which == 1:
                    once("gain", lambda: arrived(0, PASS + 2, gain_above))
            chunk.start(which)
            once("gain_sent", lambda: send(0, PASS + 2, gain, gain_above, along_x(0, below)))
        elif what == "F":
            chunk.finish(which)
        elif what == "K1":
            once("weights", lambda: wait_all(weight_loads))
            chunk.k1(which)
        elif what == "K2":
            chunk.k2(which)
        else:
            getattr(chunk.lanes[which], what)()
    for sent_q, i, src in waits:
        remote(sent_q, i, src, src, along_x(0, below)).wait_send()


def shards(streams, cotangents, feed_streams, feed_cotangents, w_in, w_out, gain):
    ticks = feed_streams.shape[0] + 1
    rows, width = streams.shape[2], streams.shape[3]
    hidden = w_in.shape[2]
    r = rows // CHUNKS
    n = SIDE * SIDE * r
    q = ticks * CHUNKS
    blocks = (q, SIDE, SIDE, r, width)
    hbm = pl.BlockSpec(memory_space=pltpu.HBM)
    vmem = pl.BlockSpec(memory_space=pltpu.VMEM)
    outs = (streams.shape, cotangents.shape, w_in.shape, w_out.shape)
    return pl.pallas_call(
        kernel,
        out_shape=tuple(pltpu.VMEM(s, F32) for s in outs),
        in_specs=[hbm] * 7,
        out_specs=(vmem,) * 4,
        scratch_shapes=[
            pltpu.VMEM((2, rows, width), F32),
            pltpu.VMEM((2, rows, width), F32),
            pltpu.VMEM(feed_streams.shape, F32),
            pltpu.VMEM(feed_cotangents.shape, F32),
            pltpu.VMEM((width, hidden), BF),
            pltpu.VMEM((hidden, width), BF),
            pltpu.VMEM((1, width), F32),
            pltpu.VMEM((1, width), F32),
            pltpu.VMEM((q, 4, r, width), F32),
            pltpu.VMEM((q - CHUNKS, 4, r, width), F32),
            pltpu.VMEM(blocks, BF),
            pltpu.VMEM(blocks, BF),
            pltpu.VMEM((q, n, hidden), BF),
            pltpu.VMEM((q, n, hidden), BF),
            pltpu.VMEM(blocks, BF),
            pltpu.VMEM(blocks, BF),
            pltpu.VMEM((q, 2, 3, SIDE, r, width), BF),
            pltpu.VMEM((CHUNKS, n, hidden), F32),
            pltpu.VMEM((CHUNKS, 2, SIDE, r, width), F32),
            pltpu.VMEM((q, 2, SIDE, r, width), BF),
            pltpu.VMEM((q, 2, 4, r, width), BF),
            pltpu.SemaphoreType.DMA((q, N_COPY)),
            pltpu.SemaphoreType.DMA((q, N_COPY)),
            pltpu.SemaphoreType.DMA((8,)),
        ],
        compiler_params=pltpu.CompilerParams(
            collective_id=0, has_side_effects=True, vmem_limit_bytes=50 * 1024 * 1024
        ),
    )(streams, cotangents, feed_streams, feed_cotangents, w_in, w_out, gain)


def solution(mesh):
    placed = (
        P("section", None, "hid", None),
        P("section", None, "hid", None),
        P(None, None, "hid", None),
        P(None, None, "hid", None),
        P("section", None, "hid"),
        P("section", "hid", None),
        P("section", None),
    )
    return jax.shard_map(
        shards,
        mesh=mesh,
        in_specs=placed,
        out_specs=(
            P("section", None, "hid", None),
            P("section", None, "hid", None),
            P("section", None, "hid"),
            P("section", "hid", None),
        ),
        check_vma=False,
    )
```

```python
from functools import partial

import jax
import jax.numpy as jnp
from jax import lax
from jax.experimental import pallas as pl
from jax.experimental.pallas import tpu as pltpu
from jax.sharding import PartitionSpec as P

MESH = pl.DeviceIdType.MESH
BF = jnp.bfloat16
F32 = jnp.float32
CHUNKS = 2
SIDE = 4
TILE = 1024
GRAD_TILE = 512
STEPS = (2, 1, -1)
LANE_COPIES = 19
RELAY_GATHER = True
RELAY_SUM = True
PASS = 2 * LANE_COPIES
N_COPY = PASS + 3
GELU_A = 0.044715
GELU_C = 0.7978845608028654


def dot_nn(a, b):
    return lax.dot_general(a, b, (((1,), (0,)), ((), ())), preferred_element_type=F32)


def dot_nt(a, b):
    return lax.dot_general(a, b, (((1,), (1,)), ((), ())), preferred_element_type=F32)


def dot_tn(a, b):
    return lax.dot_general(a, b, (((0,), (0,)), ((), ())), preferred_element_type=F32)


ORDER = (
    (0, 0, 1, "S"), (0, 0, 0, "S"), (0, 1, 1, "S"), (0, 1, 0, "S"), (0, 0, 1, "a2"), (0, 0, 0, "a2"),
    (0, 1, 1, "a2"), (0, 0, 1, "a3"), (0, 0, 0, "a3"), (0, 1, 0, "a2"), (0, 1, 1, "a3"), (0, 0, 0, "a4"),
    (0, 0, 0, "K1"), (0, 0, 0, "K2"), (0, 1, 0, "a3"), (0, 0, 1, "a4"), (0, 0, 0, "r0"), (0, 0, 1, "K1"),
    (0, 0, 1, "K2"), (0, 0, 1, "r0"), (0, 1, 0, "a4"), (0, 1, 0, "K1"), (0, 1, 0, "K2"), (0, 0, 0, "r1"),
    (0, 1, 1, "a4"), (0, 1, 0, "r0"), (0, 0, 1, "r1"), (0, 1, 1, "K1"), (0, 1, 1, "K2"), (0, 1, 1, "r0"),
    (0, 0, 0, "r2"), (0, 1, 0, "r1"), (0, 0, 1, "r2"), (0, 1, 1, "r1"), (0, 0, 0, "W"), (0, 1, 0, "r2"),
    (0, 1, 1, "r2"), (1, 0, 0, "S"), (1, 0, 1, "S"), (1, 1, 0, "S"), (1, 0, 0, "a2"), (1, 1, 1, "S"),
    (1, 0, 1, "a2"), (0, 1, 0, "W"), (1, 0, 0, "a3"), (1, 0, 1, "a3"), (1, 1, 0, "a2"), (1, 1, 1, "a2"),
    (1, 0, 0, "a4"), (1, 0, 0, "K1"), (1, 0, 0, "K2"), (1, 1, 0, "a3"), (1, 0, 0, "r0"), (1, 0, 1, "a4"),
    (1, 0, 1, "K1"), (1, 0, 1, "K2"), (1, 1, 1, "a3"), (1, 0, 1, "r0"), (1, 1, 0, "a4"), (1, 1, 0, "K1"),
    (1, 1, 0, "K2"), (1, 0, 0, "r1"), (1, 1, 1, "a4"), (1, 1, 1, "K1"), (1, 1, 0, "r0"), (1, 0, 1, "r1"),
    (1, 1, 1, "K2"), (1, 1, 1, "r0"), (1, 0, 0, "r2"), (1, 1, 0, "W"), (1, 1, 0, "r1"), (1, 0, 1, "r2"),
    (1, 1, 1, "r1"), (0, 0, 2, "W"), (1, 1, 0, "r2"), (2, 0, 0, "S"), (1, 1, 1, "r2"), (2, 0, 1, "S"),
    (2, 0, 0, "a2"), (2, 1, 0, "S"), (2, 1, 1, "S"), (2, 0, 1, "a2"), (1, 0, 2, "W"), (2, 0, 0, "a3"),
    (2, 1, 0, "a2"), (2, 0, 1, "a3"), (2, 1, 1, "a2"), (2, 0, 0, "a4"), (2, 0, 0, "K1"), (2, 0, 0, "K2"),
    (2, 1, 0, "a3"), (2, 0, 1, "a4"), (1, 0, 0, "W"), (2, 0, 0, "r0"), (2, 1, 1, "a3"), (2, 0, 1, "K1"),
    (2, 0, 1, "K2"), (2, 0, 1, "r0"), (2, 1, 0, "a4"), (2, 1, 0, "K1"), (2, 1, 0, "K2"), (2, 1, 0, "r0"),
    (2, 1, 1, "a4"), (2, 1, 1, "K1"), (2, 1, 1, "K2"), (2, 1, 1, "r0"), (0, 1, 2, "W"), (2, 0, 0, "r1"),
    (2, 0, 0, "W"), (2, 0, 1, "r1"), (2, 1, 0, "r1"), (1, 1, 2, "W"), (2, 1, 1, "r1"), (2, 0, 2, "W"),
    (2, 0, 0, "r2"), (2, 0, 1, "r2"), (2, 1, 0, "r2"), (2, 1, 1, "r2"), (2, 1, 0, "W"), (2, 1, 2, "W"),
    (2, 1, 0, "F"), (2, 0, 1, "F"), (2, 0, 0, "F"), (2, 1, 1, "F"),
)


def order(ticks):
    return ORDER


def kernel(
    streams, cots, feed_s, feed_c, w_in_hbm, w_out_hbm, gain_hbm,
    out_s, out_c, out_gin, out_gout,
    st, ct, fs, fc, w_in, w_out, gain, gain_above,
    held, got, ga, gb, hid, bpre, pa, pb,
    big_p, slope, summed, summed_b, small_r,
    ssem, rsem, lsem,
):
    ticks = feed_s.shape[0] + 1
    rows, width = st.shape[1], st.shape[2]
    r = rows // CHUNKS
    n = SIDE * SIDE * r
    sections = lax.axis_size("section")
    sec = lax.axis_index("section")
    h = lax.axis_index("hid")
    x, z = lax.rem(h, SIDE), lax.div(h, SIDE)
    top = sec == sections - 1
    below = lax.rem(sec + sections - 1, sections)
    above = lax.rem(sec + 1, sections)

    def wrap(v, by):
        return lax.rem(v + (by + SIDE), SIDE)

    def along_x(by, section=sec):
        return {"section": section, "hid": z * SIDE + wrap(x, by)}

    def along_z(by, section=sec):
        return {"section": section, "hid": wrap(z, by) * SIDE + x}

    def load(i, src, dst):
        copy = pltpu.make_async_copy(src, dst, lsem.at[i])
        copy.start()
        return copy

    first_loads = [load(0, streams.at[0], st), load(1, cots.at[0], ct), load(2, gain_hbm, gain)]
    weight_loads = [load(3, w_in_hbm.at[0], w_in), load(4, w_out_hbm.at[0], w_out)]
    feed_loads = [load(5, feed_s, fs), load(6, feed_c, fc)]

    barrier = pltpu.get_barrier_semaphore()
    peers = [axis(by, s) for s in (sec, above, below) for axis in (along_x, along_z) for by in STEPS]
    peers += [along_x(0, above), along_x(0, below)]
    for peer in peers:
        pl.semaphore_signal(barrier, inc=1, device_id=peer, device_id_type=MESH)
    pl.semaphore_wait(barrier, len(peers))
    for copy in first_loads:
        copy.wait()

    waits = []

    def remote(q, i, src, dst, dev):
        return pltpu.make_async_remote_copy(
            src_ref=src, dst_ref=dst, send_sem=ssem.at[q, i], recv_sem=rsem.at[q, i],
            device_id=dev, device_id_type=MESH,
        )

    def send(q, i, src, dst, dev):
        remote(q, i, src, dst, dev).start()
        waits.append((q, i, src))

    def arrived(q, i, dst):
        remote(q, i, dst, dst, along_x(0, below)).wait_recv()

    class Lane:
        def __init__(self, t, q, which):
            self.t, self.q, self.which = t, q, which
            if which == 0:
                self.m, self.big = x, z
                self.small_dev, self.big_dev = along_x, along_z
                self.g, self.p = ga.at[q], pa.at[q]
            else:
                self.m, self.big = z, x
                self.small_dev, self.big_dev = along_z, along_x
                self.g, self.p = gb.at[q], pb.at[q]
            self.base = which * LANE_COPIES

        def single(self, ref, big, m):
            return ref.at[big, m] if self.which == 0 else ref.at[m, big]

        def group(self, ref, big):
            return ref.at[big] if self.which == 0 else ref.at[:, big]

        def pair(self, ref, big, part):
            two = pl.ds(2 * part, 2)
            return ref.at[big, two] if self.which == 0 else ref.at[two, big]

        def send(self, i, src, dst, dev):
            send(self.q, self.base + i, src, dst, dev)

        def arrived(self, i, dst):
            arrived(self.q, self.base + i, dst)

        def a0(self):
            own = self.single(self.g, self.big, self.m)
            for i, by in enumerate(STEPS):
                self.send(i, own, own, self.small_dev(by))

        def a2(self):
            for i, by in enumerate(STEPS):
                self.arrived(i, self.single(self.g, self.big, wrap(self.m, -by)))
            if RELAY_GATHER:
                one, two = self.pair(self.g, self.big, 0), self.pair(self.g, self.big, 1)
                self.send(3, one, one, self.big_dev(1))
                self.send(4, two, two, self.big_dev(-1))
                self.send(5, two, two, self.big_dev(1))
                self.send(6, one, one, self.big_dev(-1))
            else:
                mine = self.group(self.g, self.big)
                for i, by in enumerate(STEPS):
                    self.send(3 + i, mine, mine, self.big_dev(by))

        def a3(self):
            if RELAY_GATHER:
                one = self.pair(self.g, wrap(self.big, -1), 0)
                two = self.pair(self.g, wrap(self.big, 1), 1)
                self.arrived(3, one)
                self.send(7, one, one, self.big_dev(1))
                self.arrived(4, two)
                self.send(8, two, two, self.big_dev(-1))

        def a4(self):
            if RELAY_GATHER:
                self.arrived(5, self.pair(self.g, wrap(self.big, -1), 1))
                self.arrived(6, self.pair(self.g, wrap(self.big, 1), 0))
                self.arrived(7, self.pair(self.g, wrap(self.big, 2), 0))
                self.arrived(8, self.pair(self.g, wrap(self.big, 2), 1))
            else:
                for i, by in enumerate(STEPS):
                    self.arrived(3 + i, self.group(self.g, wrap(self.big, -by)))

        def slot(self, kind, i):
            return big_p.at[self.q, self.which, 2 * kind + i]

        def r0(self):
            if RELAY_SUM:
                up, down, far = wrap(self.big, 1), wrap(self.big, -1), wrap(self.big, 2)
                self.send(9, self.pair(self.p, far, 0), self.slot(0, 0), self.big_dev(1))
                self.send(10, self.pair(self.p, far, 1), self.slot(0, 1), self.big_dev(-1))
                self.send(11, self.pair(self.p, up, 1), self.slot(1, 0), self.big_dev(1))
                self.send(12, self.pair(self.p, down, 0), self.slot(1, 1), self.big_dev(-1))
            else:
                for i, by in enumerate(STEPS):
                    self.send(
                        9 + i, self.group(self.p, wrap(self.big, by)),
                        big_r.at[self.q, self.which, i], self.big_dev(by),
                    )

        def r1(self):
            if RELAY_SUM:
                for i, by in ((0, 1), (1, -1)):
                    came, both = self.slot(0, i), self.slot(3, i)
                    self.arrived(9 + i, came)
                    own = self.pair(self.p, wrap(self.big, by), i)[...]
                    both[...] = (own.astype(F32) + came[...].astype(F32)).astype(BF)
                    self.send(13 + i, both, self.slot(2, i), self.big_dev(by))

        def r2(self):
            last = self.t == ticks - 1
            total = summed_b.at[self.q, self.which]
            keep = summed.at[self.q % CHUNKS, self.which]
            if RELAY_SUM:
                for i in (0, 1):
                    self.arrived(11 + i, self.slot(1, i))
                    self.arrived(13 + i, self.slot(2, i))
                for part in (0, 1):
                    value = (
                        self.pair(self.p, self.big, part)[...].astype(F32)
                        + self.slot(2, part)[...].astype(F32)
                        + self.slot(1, 1 - part)[...].astype(F32)
                    )
                    if last:
                        keep[pl.ds(2 * part, 2)] = value
                    total[pl.ds(2 * part, 2)] = value.astype(BF)
            else:
                value = self.group(self.p, self.big)[...].astype(F32)
                for i in range(3):
                    self.arrived(9 + i, big_r.at[self.q, self.which, i])
                    value = value + big_r[self.q, self.which, i].astype(F32)
                if last:
                    keep[...] = value
                total[...] = value.astype(BF)
            for i, by in enumerate(STEPS if last else STEPS + (0,)):
                self.send(
                    15 + i, total.at[wrap(self.m, by)],
                    small_r.at[self.q, self.which, i], self.small_dev(by, sec if last else below),
                )

        def total(self):
            last = self.t == ticks - 1
            count = 3 if last else 4
            for i in range(count):
                self.arrived(15 + i, small_r.at[self.q, self.which, i])
            parts = [small_r[self.q, self.which, i].astype(F32) for i in range(count)]
            if last:
                parts.append(summed[self.q % CHUNKS, self.which, self.m])
            return (parts[0] + parts[1]) + (parts[2] + parts[3])

    def normalized(first):
        scale_row = lax.rsqrt(jnp.mean(first * first, axis=-1, keepdims=True) + 1e-06)
        return first * scale_row, scale_row

    def grad_of(first, grad_first, back_lift, gain_row):
        normed, scale_row = normalized(first)
        back_norm = back_lift * gain_row
        back = back_norm - normed * jnp.mean(back_norm * normed, axis=-1, keepdims=True)
        return grad_first + scale_row * back

    class Chunk:
        def __init__(self, t, c, before):
            self.t, self.c, self.q, self.before = t, c, t * CHUNKS + c, before
            self.rows = pl.ds(c * r, r)
            self.lanes = (Lane(t, self.q, 0), Lane(t, self.q, 1))

        def start(self, which):
            t, q = self.t, self.q
            mine = held.at[q]
            two = pl.ds(2 * which, 2)
            if t == 0:
                mine[two] = (ct if which else st)[:, self.rows]
            else:
                last_q = self.before.q
                came = got.at[last_q]
                arrived(last_q, PASS + which, came.at[two])
                total = self.before.lanes[which].total()
                if which == 0:
                    values = (came[1] - total, came[0])
                else:
                    values = (came[3], grad_of(came[0], came[2], total, gain_above[...]))
                feed = fc if which else fs
                for i in (0, 1):
                    mine[2 * which + i] = jnp.where(top, feed[t - 1, i, self.rows], values[i])
            if which == 0:
                ga[q, z, x] = (normalized(mine[0])[0] * gain[...]).astype(BF)
            else:
                gb[q, z, x] = mine[3].astype(BF)
            self.lanes[which].a0()
            if t < ticks - 1:
                send(q, PASS + which, mine.at[two], got.at[q, two], along_x(0, below))

        def finish(self, which):
            mine = held.at[self.q]
            total = self.lanes[which].total()
            if which == 0:
                out_s[0, 0, self.rows], out_s[0, 1, self.rows] = mine[1] - total, mine[0]
            else:
                out_c[0, 0, self.rows] = mine[3]
                out_c[0, 1, self.rows] = grad_of(mine[0], mine[2], total, gain[...])

        def tiles(self, body, size):
            def step(j, carry):
                body(pl.ds(pl.multiple_of(j * TILE, TILE), TILE))
                return carry

            lax.fori_loop(0, size // TILE, step, 0)

        def k1(self, which):
            q, c = self.q, self.c

            def lifted(cols):
                pre = dot_nn(ga[q].reshape(n, width), w_in[:, cols])
                sq = pre * pre
                th = jnp.tanh(pre * (GELU_C + (GELU_C * GELU_A) * sq))
                cdf = 0.5 + 0.5 * th
                hid[q, :, cols] = (pre * cdf).astype(BF)
                slope[c, :, cols] = cdf + (0.5 * pre) * (1.0 - th * th) * (
                    GELU_C + (3.0 * GELU_C * GELU_A) * sq
                )

            def cotan(cols):
                back = dot_nt(gb[q].reshape(n, width), w_out[cols, :])
                bpre[q, :, cols] = (back * slope[c, :, cols]).astype(BF)

            self.tiles(cotan if which else lifted, w_in.shape[1])

        def k2(self, which):
            q = self.q

            def block_out(cols):
                out = dot_nn(hid[q], w_out[:, cols])
                pa[q, :, :, :, cols] = out.astype(BF).reshape(SIDE, SIDE, r, TILE)

            def back_lift(cols):
                out = dot_nt(bpre[q], w_in[cols, :])
                pb[q, :, :, :, cols] = out.astype(BF).reshape(SIDE, SIDE, r, TILE)

            self.tiles(back_lift if which else block_out, width)

    def weight_piece(t, which, lo, count):
        left, right, acc = (ga, bpre, out_gin) if which == 0 else (hid, gb, out_gout)

        def whole(ref, cols):
            if ref is ga or ref is gb:
                parts = [ref[t * CHUNKS + c, :, :, :, cols].reshape(n, -1) for c in range(CHUNKS)]
            else:
                parts = [ref[t * CHUNKS + c, :, cols] for c in range(CHUNKS)]
            return jnp.concatenate(parts, axis=0)

        def body(j, carry):
            cols = pl.ds(pl.multiple_of(j * GRAD_TILE, GRAD_TILE), GRAD_TILE)
            part = dot_tn(whole(left, cols), whole(right, pl.ds(0, width)))
            acc[0, cols, :] = part if t == 0 else acc[0, cols, :] + part
            return carry

        first = lo * 256 // GRAD_TILE
        lax.fori_loop(first, first + count * 256 // GRAD_TILE, body, 0)

    chunks = {}
    for t in range(ticks):
        for c in range(CHUNKS):
            chunks[t, c] = Chunk(t, c, chunks.get((t - 1, c)))
    pending = {}

    def once(key, run):
        if key not in pending:
            pending[key] = True
            run()

    def wait_all(copies):
        for copy in copies:
            copy.wait()

    for t, c, which, what in order(ticks):
        if what == "W":
            weight_piece(t, c, which, 2)
            continue
        chunk = chunks[t, c]
        if what == "S":
            if t > 0:
                once("feed", lambda: wait_all(feed_loads))
                if which == 1:
                    once("gain", lambda: arrived(0, PASS + 2, gain_above))
            chunk.start(which)
            once("gain_sent", lambda: send(0, PASS + 2, gain, gain_above, along_x(0, below)))
        elif what == "F":
            chunk.finish(which)
        elif what == "K1":
            once("weights", lambda: wait_all(weight_loads))
            chunk.k1(which)
        elif what == "K2":
            chunk.k2(which)
        else:
            getattr(chunk.lanes[which], what)()
    for sent_q, i, src in waits:
        remote(sent_q, i, src, src, along_x(0, below)).wait_send()


def shards(streams, cotangents, feed_streams, feed_cotangents, w_in, w_out, gain):
    ticks = feed_streams.shape[0] + 1
    rows, width = streams.shape[2], streams.shape[3]
    hidden = w_in.shape[2]
    r = rows // CHUNKS
    n = SIDE * SIDE * r
    q = ticks * CHUNKS
    blocks = (q, SIDE, SIDE, r, width)
    hbm = pl.BlockSpec(memory_space=pltpu.HBM)
    vmem = pl.BlockSpec(memory_space=pltpu.VMEM)
    outs = (streams.shape, cotangents.shape, w_in.shape, w_out.shape)
    held_outs = pl.pallas_call(
        kernel,
        out_shape=tuple(pltpu.VMEM(s, F32) for s in outs),
        in_specs=[hbm] * 7,
        out_specs=(vmem,) * 4,
        scratch_shapes=[
            pltpu.VMEM((2, rows, width), F32),
            pltpu.VMEM((2, rows, width), F32),
            pltpu.VMEM(feed_streams.shape, F32),
            pltpu.VMEM(feed_cotangents.shape, F32),
            pltpu.VMEM((width, hidden), BF),
            pltpu.VMEM((hidden, width), BF),
            pltpu.VMEM((1, width), F32),
            pltpu.VMEM((1, width), F32),
            pltpu.VMEM((q, 4, r, width), F32),
            pltpu.VMEM((q - CHUNKS, 4, r, width), F32),
            pltpu.VMEM(blocks, BF),
            pltpu.VMEM(blocks, BF),
            pltpu.VMEM((q, n, hidden), BF),
            pltpu.VMEM((q, n, hidden), BF),
            pltpu.VMEM(blocks, BF),
            pltpu.VMEM(blocks, BF),
            pltpu.VMEM((q, 2, 8, 2, r, width), BF),
            pltpu.VMEM((CHUNKS, n, hidden), F32),
            pltpu.VMEM((CHUNKS, 2, SIDE, r, width), F32),
            pltpu.VMEM((q, 2, SIDE, r, width), BF),
            pltpu.VMEM((q, 2, 4, r, width), BF),
            pltpu.SemaphoreType.DMA((q, N_COPY)),
            pltpu.SemaphoreType.DMA((q, N_COPY)),
            pltpu.SemaphoreType.DMA((8,)),
        ],
        compiler_params=pltpu.CompilerParams(
            collective_id=0, has_side_effects=True, vmem_limit_bytes=50 * 1024 * 1024
        ),
    )(streams, cotangents, feed_streams, feed_cotangents, w_in, w_out, gain)
    parts = [(2, k) for k in range(4)] + [(3, k) for k in range(4)] + [(0, 0), (1, 0)]

    def store(*refs):
        outs_in, outs_to, sems = refs[:4], refs[4:8], refs[8]
        copies = []
        for i, (which, k) in enumerate(parts):
            src, dst = outs_in[which].at[0], outs_to[which].at[0]
            if which >= 2:
                span = pl.ds(k * (src.shape[0] // 4), src.shape[0] // 4)
                src, dst = src.at[span], dst.at[span]
            copies.append(pltpu.make_async_copy(src, dst, sems.at[i]))
            copies[-1].start()
        for copy in copies:
            copy.wait()

    return pl.pallas_call(
        store,
        out_shape=tuple(jax.ShapeDtypeStruct(s, F32) for s in outs),
        in_specs=[vmem] * 4,
        out_specs=(hbm,) * 4,
        scratch_shapes=[pltpu.SemaphoreType.DMA((len(parts),))],
        compiler_params=pltpu.CompilerParams(vmem_limit_bytes=4 * 1024 * 1024),
    )(*[pltpu.with_memory_space_constraint(a, pltpu.VMEM) for a in held_outs])


def solution(mesh):
    placed = (
        P("section", None, "hid", None),
        P("section", None, "hid", None),
        P(None, None, "hid", None),
        P(None, None, "hid", None),
        P("section", None, "hid"),
        P("section", "hid", None),
        P("section", None),
    )
    return jax.shard_map(
        shards,
        mesh=mesh,
        in_specs=placed,
        out_specs=(
            P("section", None, "hid", None),
            P("section", None, "hid", None),
            P("section", None, "hid"),
            P("section", "hid", None),
        ),
        check_vma=False,
    )
```

```python
from functools import partial

import jax
import jax.numpy as jnp
from jax import lax
from jax.experimental import pallas as pl
from jax.experimental.pallas import tpu as pltpu
from jax.sharding import PartitionSpec as P

MESH = pl.DeviceIdType.MESH
BF = jnp.bfloat16
F32 = jnp.float32
CHUNKS = 2
SIDE = 4
TILE = 1024
GRAD_TILE = 512
STEPS = (2, 1, -1)
LANE_COPIES = 19
RELAY_GATHER = True
RELAY_SUM = True
PASS = 2 * LANE_COPIES
N_COPY = PASS + 3
GELU_A = 0.044715
GELU_C = 0.7978845608028654


def dot_nn(a, b):
    return lax.dot_general(a, b, (((1,), (0,)), ((), ())), preferred_element_type=F32)


def dot_nt(a, b):
    return lax.dot_general(a, b, (((1,), (1,)), ((), ())), preferred_element_type=F32)


def dot_tn(a, b):
    return lax.dot_general(a, b, (((0,), (0,)), ((), ())), preferred_element_type=F32)


ORDER = (
    (0, 0, 0, "S"), (0, 1, 0, "S"), (0, 0, 1, "S"), (0, 1, 1, "S"), (0, 0, 0, "a2"), (0, 0, 1, "a2"),
    (0, 0, 0, "a3"), (0, 1, 0, "a2"), (0, 0, 1, "a3"), (0, 1, 1, "a2"), (0, 0, 0, "a4"), (0, 0, 0, "K1"),
    (0, 0, 0, "K2"), (0, 1, 0, "a3"), (0, 0, 0, "r0"), (0, 1, 1, "a3"), (0, 0, 1, "a4"), (0, 0, 1, "K1"),
    (0, 0, 1, "K2"), (0, 0, 1, "r0"), (0, 1, 0, "a4"), (0, 1, 0, "K1"), (0, 1, 0, "K2"), (0, 0, 0, "r1"),
    (0, 1, 1, "a4"), (0, 1, 0, "r0"), (0, 1, 1, "K1"), (0, 0, 1, "r1"), (0, 1, 1, "K2"), (0, 1, 1, "r0"),
    (0, 0, 0, "r2"), (0, 1, 0, "r1"), (0, 0, 2, "W"), (0, 1, 1, "r1"), (0, 0, 1, "r2"), (0, 1, 0, "r2"),
    (0, 1, 0, "W"), (1, 0, 0, "S"), (0, 1, 1, "r2"), (1, 0, 1, "S"), (0, 1, 2, "W"), (1, 0, 0, "a2"),
    (1, 1, 0, "S"), (1, 0, 1, "a2"), (1, 1, 1, "S"), (1, 0, 0, "a3"), (1, 1, 0, "a2"), (1, 0, 1, "a3"),
    (1, 1, 1, "a2"), (1, 0, 0, "a4"), (1, 0, 0, "K1"), (1, 0, 0, "K2"), (1, 1, 0, "a3"), (1, 0, 0, "r0"),
    (1, 0, 1, "a4"), (1, 0, 1, "K1"), (1, 1, 1, "a3"), (1, 0, 1, "K2"), (1, 0, 1, "r0"), (1, 1, 0, "a4"),
    (1, 1, 0, "K1"), (1, 1, 0, "K2"), (1, 0, 0, "r1"), (1, 1, 1, "a4"), (1, 1, 0, "r0"), (1, 1, 1, "K1"),
    (1, 0, 1, "r1"), (1, 1, 1, "K2"), (1, 1, 1, "r0"), (1, 0, 0, "r2"), (1, 1, 0, "r1"), (1, 0, 1, "r2"),
    (1, 1, 1, "r1"), (1, 1, 0, "r2"), (2, 0, 0, "S"), (1, 1, 1, "r2"), (2, 0, 1, "S"), (2, 1, 0, "S"),
    (2, 0, 0, "a2"), (1, 0, 2, "W"), (2, 1, 1, "S"), (2, 0, 1, "a2"), (2, 0, 0, "a3"), (1, 1, 2, "W"),
    (2, 1, 0, "a2"), (2, 0, 1, "a3"), (1, 1, 0, "W"), (2, 1, 1, "a2"), (2, 0, 0, "a4"), (2, 0, 0, "K1"),
    (2, 0, 0, "K2"), (2, 1, 0, "a3"), (2, 0, 1, "a4"), (2, 0, 1, "K1"), (2, 1, 1, "a3"), (2, 0, 0, "r0"),
    (2, 0, 1, "K2"), (2, 0, 1, "r0"), (2, 1, 0, "a4"), (2, 1, 0, "K1"), (2, 1, 0, "K2"), (2, 1, 0, "r0"),
    (2, 1, 1, "a4"), (2, 1, 1, "K1"), (2, 1, 1, "K2"), (2, 1, 1, "r0"), (0, 0, 0, "W"), (2, 0, 1, "r1"),
    (2, 0, 0, "r1"), (2, 0, 2, "W"), (2, 1, 0, "r1"), (2, 1, 0, "W"), (2, 1, 1, "r1"), (2, 0, 0, "r2"),
    (2, 1, 2, "W"), (2, 0, 1, "r2"), (2, 1, 0, "r2"), (2, 1, 1, "r2"), (1, 0, 0, "W"), (2, 0, 0, "W"),
    (2, 0, 0, "F"), (2, 1, 0, "F"), (2, 0, 1, "F"), (2, 1, 1, "F"),
)


def order(ticks):
    return ORDER


def kernel(
    streams, cots, feed_s, feed_c, w_in_hbm, w_out_hbm, gain_hbm,
    out_s, out_c, out_gin, out_gout,
    st, ct, fs, fc, w_in, w_out, gain, gain_above,
    held, got, ga, gb, hid, bpre, pa, pb,
    big_p, slope, summed, summed_b, small_r,
    ssem, rsem, lsem,
):
    ticks = feed_s.shape[0] + 1
    rows, width = st.shape[1], st.shape[2]
    r = rows // CHUNKS
    n = SIDE * SIDE * r
    sections = lax.axis_size("section")
    sec = lax.axis_index("section")
    h = lax.axis_index("hid")
    x, z = lax.rem(h, SIDE), lax.div(h, SIDE)
    top = sec == sections - 1
    below = lax.rem(sec + sections - 1, sections)
    above = lax.rem(sec + 1, sections)

    def wrap(v, by):
        return lax.rem(v + (by + SIDE), SIDE)

    def along_x(by, section=sec):
        return {"section": section, "hid": z * SIDE + wrap(x, by)}

    def along_z(by, section=sec):
        return {"section": section, "hid": wrap(z, by) * SIDE + x}

    def load(i, src, dst):
        copy = pltpu.make_async_copy(src, dst, lsem.at[i])
        copy.start()
        return copy

    first_loads = [load(0, streams.at[0], st), load(1, cots.at[0], ct), load(2, gain_hbm, gain)]

    barrier = pltpu.get_barrier_semaphore()
    peers = [axis(by, s) for s in (sec, above, below) for axis in (along_x, along_z) for by in STEPS]
    peers += [along_x(0, above), along_x(0, below)]
    for peer in peers:
        pl.semaphore_signal(barrier, inc=1, device_id=peer, device_id_type=MESH)
    for copy in first_loads:
        copy.wait()

    waits = []

    def remote(q, i, src, dst, dev):
        return pltpu.make_async_remote_copy(
            src_ref=src, dst_ref=dst, send_sem=ssem.at[q, i], recv_sem=rsem.at[q, i],
            device_id=dev, device_id_type=MESH,
        )

    def send(q, i, src, dst, dev):
        remote(q, i, src, dst, dev).start()
        waits.append((q, i, src))

    def arrived(q, i, dst):
        remote(q, i, dst, dst, along_x(0, below)).wait_recv()

    class Lane:
        def __init__(self, t, q, which):
            self.t, self.q, self.which = t, q, which
            if which == 0:
                self.m, self.big = x, z
                self.small_dev, self.big_dev = along_x, along_z
                self.g, self.p = ga.at[q], pa.at[q]
            else:
                self.m, self.big = z, x
                self.small_dev, self.big_dev = along_z, along_x
                self.g, self.p = gb.at[q], pb.at[q]
            self.base = which * LANE_COPIES

        def single(self, ref, big, m):
            return ref.at[big, m] if self.which == 0 else ref.at[m, big]

        def group(self, ref, big):
            return ref.at[big] if self.which == 0 else ref.at[:, big]

        def pair(self, ref, big, part):
            two = pl.ds(2 * part, 2)
            return ref.at[big, two] if self.which == 0 else ref.at[two, big]

        def send(self, i, src, dst, dev):
            send(self.q, self.base + i, src, dst, dev)

        def arrived(self, i, dst):
            arrived(self.q, self.base + i, dst)

        def a0(self):
            own = self.single(self.g, self.big, self.m)
            for i, by in enumerate(STEPS):
                self.send(i, own, own, self.small_dev(by))

        def a2(self):
            for i, by in enumerate(STEPS):
                self.arrived(i, self.single(self.g, self.big, wrap(self.m, -by)))
            if RELAY_GATHER:
                one, two = self.pair(self.g, self.big, 0), self.pair(self.g, self.big, 1)
                self.send(3, one, one, self.big_dev(1))
                self.send(4, two, two, self.big_dev(-1))
                self.send(5, two, two, self.big_dev(1))
                self.send(6, one, one, self.big_dev(-1))
            else:
                mine = self.group(self.g, self.big)
                for i, by in enumerate(STEPS):
                    self.send(3 + i, mine, mine, self.big_dev(by))

        def a3(self):
            if RELAY_GATHER:
                one = self.pair(self.g, wrap(self.big, -1), 0)
                two = self.pair(self.g, wrap(self.big, 1), 1)
                self.arrived(3, one)
                self.send(7, one, one, self.big_dev(1))
                self.arrived(4, two)
                self.send(8, two, two, self.big_dev(-1))

        def a4(self):
            if RELAY_GATHER:
                self.arrived(5, self.pair(self.g, wrap(self.big, -1), 1))
                self.arrived(6, self.pair(self.g, wrap(self.big, 1), 0))
                self.arrived(7, self.pair(self.g, wrap(self.big, 2), 0))
                self.arrived(8, self.pair(self.g, wrap(self.big, 2), 1))
            else:
                for i, by in enumerate(STEPS):
                    self.arrived(3 + i, self.group(self.g, wrap(self.big, -by)))

        def slot(self, kind, i):
            return big_p.at[self.q, self.which, 2 * kind + i]

        def r0(self):
            if RELAY_SUM:
                up, down, far = wrap(self.big, 1), wrap(self.big, -1), wrap(self.big, 2)
                self.send(9, self.pair(self.p, far, 0), self.slot(0, 0), self.big_dev(1))
                self.send(10, self.pair(self.p, far, 1), self.slot(0, 1), self.big_dev(-1))
                self.send(11, self.pair(self.p, up, 1), self.slot(1, 0), self.big_dev(1))
                self.send(12, self.pair(self.p, down, 0), self.slot(1, 1), self.big_dev(-1))
            else:
                for i, by in enumerate(STEPS):
                    self.send(
                        9 + i, self.group(self.p, wrap(self.big, by)),
                        big_r.at[self.q, self.which, i], self.big_dev(by),
                    )

        def r1(self):
            if RELAY_SUM:
                for i, by in ((0, 1), (1, -1)):
                    came, both = self.slot(0, i), self.slot(3, i)
                    self.arrived(9 + i, came)
                    own = self.pair(self.p, wrap(self.big, by), i)[...]
                    both[...] = (own.astype(F32) + came[...].astype(F32)).astype(BF)
                    self.send(13 + i, both, self.slot(2, i), self.big_dev(by))

        def r2(self):
            last = self.t == ticks - 1
            total = summed_b.at[self.q, self.which]
            keep = summed.at[self.q % CHUNKS, self.which]
            if RELAY_SUM:
                for i in (0, 1):
                    self.arrived(11 + i, self.slot(1, i))
                    self.arrived(13 + i, self.slot(2, i))
                for part in (0, 1):
                    value = (
                        self.pair(self.p, self.big, part)[...].astype(F32)
                        + self.slot(2, part)[...].astype(F32)
                        + self.slot(1, 1 - part)[...].astype(F32)
                    )
                    if last:
                        keep[pl.ds(2 * part, 2)] = value
                    total[pl.ds(2 * part, 2)] = value.astype(BF)
            else:
                value = self.group(self.p, self.big)[...].astype(F32)
                for i in range(3):
                    self.arrived(9 + i, big_r.at[self.q, self.which, i])
                    value = value + big_r[self.q, self.which, i].astype(F32)
                if last:
                    keep[...] = value
                total[...] = value.astype(BF)
            for i, by in enumerate(STEPS if last else STEPS + (0,)):
                self.send(
                    15 + i, total.at[wrap(self.m, by)],
                    small_r.at[self.q, self.which, i], self.small_dev(by, sec if last else below),
                )

        def total(self):
            last = self.t == ticks - 1
            count = 3 if last else 4
            for i in range(count):
                self.arrived(15 + i, small_r.at[self.q, self.which, i])
            parts = [small_r[self.q, self.which, i].astype(F32) for i in range(count)]
            if last:
                parts.append(summed[self.q % CHUNKS, self.which, self.m])
            return (parts[0] + parts[1]) + (parts[2] + parts[3])

    def normalized(first):
        scale_row = lax.rsqrt(jnp.mean(first * first, axis=-1, keepdims=True) + 1e-06)
        return first * scale_row, scale_row

    def grad_of(first, grad_first, back_lift, gain_row):
        normed, scale_row = normalized(first)
        back_norm = back_lift * gain_row
        back = back_norm - normed * jnp.mean(back_norm * normed, axis=-1, keepdims=True)
        return grad_first + scale_row * back

    class Chunk:
        def __init__(self, t, c, before):
            self.t, self.c, self.q, self.before = t, c, t * CHUNKS + c, before
            self.rows = pl.ds(c * r, r)
            self.lanes = (Lane(t, self.q, 0), Lane(t, self.q, 1))

        def prepare(self, which):
            t, q = self.t, self.q
            mine = held.at[q]
            two = pl.ds(2 * which, 2)
            if t == 0:
                mine[two] = (ct if which else st)[:, self.rows]
            else:
                last_q = self.before.q
                came = got.at[last_q]
                arrived(last_q, PASS + which, came.at[two])
                total = self.before.lanes[which].total()
                if which == 0:
                    values = (came[1] - total, came[0])
                else:
                    values = (came[3], grad_of(came[0], came[2], total, gain_above[...]))
                feed = fc if which else fs
                for i in (0, 1):
                    mine[2 * which + i] = jnp.where(top, feed[t - 1, i, self.rows], values[i])
            if which == 0:
                ga[q, z, x] = (normalized(mine[0])[0] * gain[...]).astype(BF)
            else:
                gb[q, z, x] = mine[3].astype(BF)

        def start(self, which):
            t, q = self.t, self.q
            two = pl.ds(2 * which, 2)
            if t > 0:
                self.prepare(which)
            self.lanes[which].a0()
            if t < ticks - 1:
                send(q, PASS + which, held.at[q, two], got.at[q, two], along_x(0, below))

        def finish(self, which):
            mine = held.at[self.q]
            total = self.lanes[which].total()
            if which == 0:
                out_s[0, 0, self.rows], out_s[0, 1, self.rows] = mine[1] - total, mine[0]
            else:
                out_c[0, 0, self.rows] = mine[3]
                out_c[0, 1, self.rows] = grad_of(mine[0], mine[2], total, gain[...])

        def tiles(self, body, size):
            def step(j, carry):
                body(pl.ds(pl.multiple_of(j * TILE, TILE), TILE))
                return carry

            lax.fori_loop(0, size // TILE, step, 0)

        def k1(self, which):
            q, c = self.q, self.c

            def lifted(cols):
                pre = dot_nn(ga[q].reshape(n, width), w_in[:, cols])
                sq = pre * pre
                th = jnp.tanh(pre * (GELU_C + (GELU_C * GELU_A) * sq))
                cdf = 0.5 + 0.5 * th
                hid[q, :, cols] = (pre * cdf).astype(BF)
                slope[c, :, cols] = cdf + (0.5 * pre) * (1.0 - th * th) * (
                    GELU_C + (3.0 * GELU_C * GELU_A) * sq
                )

            def cotan(cols):
                back = dot_nt(gb[q].reshape(n, width), w_out[cols, :])
                bpre[q, :, cols] = (back * slope[c, :, cols]).astype(BF)

            self.tiles(cotan if which else lifted, w_in.shape[1])

        def k2(self, which):
            q = self.q

            def block_out(cols):
                out = dot_nn(hid[q], w_out[:, cols])
                pa[q, :, :, :, cols] = out.astype(BF).reshape(SIDE, SIDE, r, TILE)

            def back_lift(cols):
                out = dot_nt(bpre[q], w_in[cols, :])
                pb[q, :, :, :, cols] = out.astype(BF).reshape(SIDE, SIDE, r, TILE)

            self.tiles(back_lift if which else block_out, width)

    def weight_piece(t, which, lo, count):
        left, right, acc = (ga, bpre, out_gin) if which == 0 else (hid, gb, out_gout)

        def whole(ref, cols):
            if ref is ga or ref is gb:
                parts = [ref[t * CHUNKS + c, :, :, :, cols].reshape(n, -1) for c in range(CHUNKS)]
            else:
                parts = [ref[t * CHUNKS + c, :, cols] for c in range(CHUNKS)]
            return jnp.concatenate(parts, axis=0)

        def body(j, carry):
            cols = pl.ds(pl.multiple_of(j * GRAD_TILE, GRAD_TILE), GRAD_TILE)
            part = dot_tn(whole(left, cols), whole(right, pl.ds(0, width)))
            acc[0, cols, :] = part if t == 0 else acc[0, cols, :] + part
            return carry

        first = lo * 256 // GRAD_TILE
        lax.fori_loop(first, first + count * 256 // GRAD_TILE, body, 0)

    chunks = {}
    for t in range(ticks):
        for c in range(CHUNKS):
            chunks[t, c] = Chunk(t, c, chunks.get((t - 1, c)))
    pending = {}

    def once(key, run):
        if key not in pending:
            pending[key] = True
            run()

    def wait_all(copies):
        for copy in copies:
            copy.wait()

    for c in range(CHUNKS):
        for which in (0, 1):
            chunks[0, c].prepare(which)
    pl.semaphore_wait(barrier, len(peers))
    later = []

    def load_rest():
        later.extend([load(3, w_in_hbm.at[0], w_in), load(4, w_out_hbm.at[0], w_out)])
        later.extend([load(5, feed_s, fs), load(6, feed_c, fc)])

    for t, c, which, what in order(ticks):
        if what != "S":
            once("rest", load_rest)
        if what == "W":
            weight_piece(t, c, which, 2)
            continue
        chunk = chunks[t, c]
        if what == "S":
            if t > 0:
                once("feed", lambda: wait_all(later[2:]))
                if which == 1:
                    once("gain", lambda: arrived(0, PASS + 2, gain_above))
            chunk.start(which)
            once("gain_sent", lambda: send(0, PASS + 2, gain, gain_above, along_x(0, below)))
        elif what == "F":
            chunk.finish(which)
        elif what == "K1":
            once("weights", lambda: wait_all(later[:2]))
            chunk.k1(which)
        elif what == "K2":
            chunk.k2(which)
        else:
            getattr(chunk.lanes[which], what)()
    for sent_q, i, src in waits:
        remote(sent_q, i, src, src, along_x(0, below)).wait_send()


def shards(streams, cotangents, feed_streams, feed_cotangents, w_in, w_out, gain):
    ticks = feed_streams.shape[0] + 1
    rows, width = streams.shape[2], streams.shape[3]
    hidden = w_in.shape[2]
    r = rows // CHUNKS
    n = SIDE * SIDE * r
    q = ticks * CHUNKS
    blocks = (q, SIDE, SIDE, r, width)
    hbm = pl.BlockSpec(memory_space=pltpu.HBM)
    vmem = pl.BlockSpec(memory_space=pltpu.VMEM)
    outs = (streams.shape, cotangents.shape, w_in.shape, w_out.shape)
    held_outs = pl.pallas_call(
        kernel,
        out_shape=tuple(pltpu.VMEM(s, F32) for s in outs),
        in_specs=[hbm] * 7,
        out_specs=(vmem,) * 4,
        scratch_shapes=[
            pltpu.VMEM((2, rows, width), F32),
            pltpu.VMEM((2, rows, width), F32),
            pltpu.VMEM(feed_streams.shape, F32),
            pltpu.VMEM(feed_cotangents.shape, F32),
            pltpu.VMEM((width, hidden), BF),
            pltpu.VMEM((hidden, width), BF),
            pltpu.VMEM((1, width), F32),
            pltpu.VMEM((1, width), F32),
            pltpu.VMEM((q, 4, r, width), F32),
            pltpu.VMEM((q - CHUNKS, 4, r, width), F32),
            pltpu.VMEM(blocks, BF),
            pltpu.VMEM(blocks, BF),
            pltpu.VMEM((q, n, hidden), BF),
            pltpu.VMEM((q, n, hidden), BF),
            pltpu.VMEM(blocks, BF),
            pltpu.VMEM(blocks, BF),
            pltpu.VMEM((q, 2, 8, 2, r, width), BF),
            pltpu.VMEM((CHUNKS, n, hidden), F32),
            pltpu.VMEM((CHUNKS, 2, SIDE, r, width), F32),
            pltpu.VMEM((q, 2, SIDE, r, width), BF),
            pltpu.VMEM((q, 2, 4, r, width), BF),
            pltpu.SemaphoreType.DMA((q, N_COPY)),
            pltpu.SemaphoreType.DMA((q, N_COPY)),
            pltpu.SemaphoreType.DMA((8,)),
        ],
        compiler_params=pltpu.CompilerParams(
            collective_id=0, has_side_effects=True, vmem_limit_bytes=50 * 1024 * 1024
        ),
    )(streams, cotangents, feed_streams, feed_cotangents, w_in, w_out, gain)
    parts = [(2, k) for k in range(4)] + [(3, k) for k in range(4)] + [(0, 0), (1, 0)]

    def store(*refs):
        outs_in, outs_to, sems = refs[:4], refs[4:8], refs[8]
        copies = []
        for i, (which, k) in enumerate(parts):
            src, dst = outs_in[which].at[0], outs_to[which].at[0]
            if which >= 2:
                span = pl.ds(k * (src.shape[0] // 4), src.shape[0] // 4)
                src, dst = src.at[span], dst.at[span]
            copies.append(pltpu.make_async_copy(src, dst, sems.at[i]))
            copies[-1].start()
        for copy in copies:
            copy.wait()

    return pl.pallas_call(
        store,
        out_shape=tuple(jax.ShapeDtypeStruct(s, F32) for s in outs),
        in_specs=[vmem] * 4,
        out_specs=(hbm,) * 4,
        scratch_shapes=[pltpu.SemaphoreType.DMA((len(parts),))],
        compiler_params=pltpu.CompilerParams(vmem_limit_bytes=4 * 1024 * 1024),
    )(*[pltpu.with_memory_space_constraint(a, pltpu.VMEM) for a in held_outs])


def solution(mesh):
    placed = (
        P("section", None, "hid", None),
        P("section", None, "hid", None),
        P(None, None, "hid", None),
        P(None, None, "hid", None),
        P("section", None, "hid"),
        P("section", "hid", None),
        P("section", None),
    )
    return jax.shard_map(
        shards,
        mesh=mesh,
        in_specs=placed,
        out_specs=(
            P("section", None, "hid", None),
            P("section", None, "hid", None),
            P("section", None, "hid"),
            P("section", "hid", None),
        ),
        check_vma=False,
    )
```

```python
from functools import partial

import jax
import jax.numpy as jnp
from jax import lax
from jax.experimental import pallas as pl
from jax.experimental.pallas import tpu as pltpu
from jax.sharding import PartitionSpec as P

MESH = pl.DeviceIdType.MESH
BF = jnp.bfloat16
F32 = jnp.float32
CHUNKS = 2
SIDE = 4
TILE = 1024
GRAD_TILE = 512
STEPS = (2, 1, -1)
LANE_COPIES = 19
RELAY_GATHER = True
RELAY_SUM = True
PASS = 2 * LANE_COPIES
N_COPY = PASS + 3
GELU_A = 0.044715
GELU_C = 0.7978845608028654


def dot_nn(a, b):
    return lax.dot_general(a, b, (((1,), (0,)), ((), ())), preferred_element_type=F32)


def dot_nt(a, b):
    return lax.dot_general(a, b, (((1,), (1,)), ((), ())), preferred_element_type=F32)


def dot_tn(a, b):
    return lax.dot_general(a, b, (((0,), (0,)), ((), ())), preferred_element_type=F32)


ORDER = (
    (0, 0, 0, "S"), (0, 1, 0, "S"), (0, 0, 1, "S"), (0, 1, 1, "S"), (0, 0, 0, "a2"), (0, 0, 1, "a2"),
    (0, 0, 0, "a3"), (0, 1, 0, "a2"), (0, 0, 1, "a3"), (0, 1, 1, "a2"), (0, 0, 0, "a4"), (0, 0, 0, "K1"),
    (0, 0, 0, "K2"), (0, 1, 0, "a3"), (0, 0, 0, "r0"), (0, 1, 1, "a3"), (0, 0, 1, "a4"), (0, 0, 1, "K1"),
    (0, 0, 1, "K2"), (0, 0, 1, "r0"), (0, 1, 0, "a4"), (0, 1, 0, "K1"), (0, 1, 0, "K2"), (0, 0, 0, "r1"),
    (0, 1, 1, "a4"), (0, 1, 0, "r0"), (0, 1, 1, "K1"), (0, 0, 1, "r1"), (0, 1, 1, "K2"), (0, 1, 1, "r0"),
    (0, 0, 0, "r2"), (0, 1, 0, "r1"), (0, 0, 2, "W"), (0, 1, 1, "r1"), (0, 0, 1, "r2"), (0, 1, 0, "r2"),
    (0, 1, 0, "W"), (1, 0, 0, "S"), (0, 1, 1, "r2"), (1, 0, 1, "S"), (0, 1, 2, "W"), (1, 0, 0, "a2"),
    (1, 1, 0, "S"), (1, 0, 1, "a2"), (1, 1, 1, "S"), (1, 0, 0, "a3"), (1, 1, 0, "a2"), (1, 0, 1, "a3"),
    (1, 1, 1, "a2"), (1, 0, 0, "a4"), (1, 0, 0, "K1"), (1, 0, 0, "K2"), (1, 1, 0, "a3"), (1, 0, 0, "r0"),
    (1, 0, 1, "a4"), (1, 0, 1, "K1"), (1, 1, 1, "a3"), (1, 0, 1, "K2"), (1, 0, 1, "r0"), (1, 1, 0, "a4"),
    (1, 1, 0, "K1"), (1, 1, 0, "K2"), (1, 0, 0, "r1"), (1, 1, 1, "a4"), (1, 1, 0, "r0"), (1, 1, 1, "K1"),
    (1, 0, 1, "r1"), (1, 1, 1, "K2"), (1, 1, 1, "r0"), (1, 0, 0, "r2"), (1, 1, 0, "r1"), (1, 0, 1, "r2"),
    (1, 1, 1, "r1"), (1, 1, 0, "r2"), (2, 0, 0, "S"), (1, 1, 1, "r2"), (2, 0, 1, "S"), (2, 1, 0, "S"),
    (2, 0, 0, "a2"), (1, 0, 2, "W"), (2, 1, 1, "S"), (2, 0, 1, "a2"), (2, 0, 0, "a3"), (1, 1, 2, "W"),
    (2, 1, 0, "a2"), (2, 0, 1, "a3"), (1, 1, 0, "W"), (2, 1, 1, "a2"), (2, 0, 0, "a4"), (2, 0, 0, "K1"),
    (2, 0, 0, "K2"), (2, 1, 0, "a3"), (2, 0, 1, "a4"), (2, 0, 1, "K1"), (2, 1, 1, "a3"), (2, 0, 0, "r0"),
    (2, 0, 1, "K2"), (2, 0, 1, "r0"), (2, 1, 0, "a4"), (2, 1, 0, "K1"), (2, 1, 0, "K2"), (2, 1, 0, "r0"),
    (2, 1, 1, "a4"), (2, 1, 1, "K1"), (2, 1, 1, "K2"), (2, 1, 1, "r0"), (0, 0, 0, "W"), (2, 0, 1, "r1"),
    (2, 0, 0, "r1"), (2, 0, 2, "W"), (2, 1, 0, "r1"), (2, 1, 0, "W"), (2, 1, 1, "r1"), (2, 0, 0, "r2"),
    (2, 1, 2, "W"), (2, 0, 1, "r2"), (2, 1, 0, "r2"), (2, 1, 1, "r2"), (1, 0, 0, "W"), (2, 0, 0, "W"),
    (2, 0, 0, "F"), (2, 1, 0, "F"), (2, 0, 1, "F"), (2, 1, 1, "F"),
)


def order(ticks):
    return ORDER


def kernel(
    streams, cots, feed_s, feed_c, w_in_hbm, w_out_hbm, gain_hbm,
    out_s, out_c, out_gin, out_gout,
    st, ct, fs, fc, w_in, w_out, gain, gain_above,
    held, got, ga, gb, hid, bpre, pa, pb,
    big_p, slope, summed, summed_b, small_r,
    ssem, rsem, lsem,
):
    ticks = feed_s.shape[0] + 1
    rows, width = st.shape[1], st.shape[2]
    r = rows // CHUNKS
    n = SIDE * SIDE * r
    sections = lax.axis_size("section")
    sec = lax.axis_index("section")
    h = lax.axis_index("hid")
    x, z = lax.rem(h, SIDE), lax.div(h, SIDE)
    top = sec == sections - 1
    below = lax.rem(sec + sections - 1, sections)
    above = lax.rem(sec + 1, sections)

    def wrap(v, by):
        return lax.rem(v + (by + SIDE), SIDE)

    def along_x(by, section=sec):
        return {"section": section, "hid": z * SIDE + wrap(x, by)}

    def along_z(by, section=sec):
        return {"section": section, "hid": wrap(z, by) * SIDE + x}

    def load(i, src, dst):
        copy = pltpu.make_async_copy(src, dst, lsem.at[i])
        copy.start()
        return copy

    first_loads = [load(0, streams.at[0], st), load(1, cots.at[0], ct), load(2, gain_hbm, gain)]

    barrier = pltpu.get_barrier_semaphore()
    peers = [axis(by, s) for s in (sec, above, below) for axis in (along_x, along_z) for by in STEPS]
    peers += [along_x(0, above), along_x(0, below)]
    for peer in peers:
        pl.semaphore_signal(barrier, inc=1, device_id=peer, device_id_type=MESH)
    for copy in first_loads:
        copy.wait()

    waits = []

    def remote(q, i, src, dst, dev):
        return pltpu.make_async_remote_copy(
            src_ref=src, dst_ref=dst, send_sem=ssem.at[q, i], recv_sem=rsem.at[q, i],
            device_id=dev, device_id_type=MESH,
        )

    def send(q, i, src, dst, dev):
        remote(q, i, src, dst, dev).start()
        waits.append((q, i, src))

    def arrived(q, i, dst):
        remote(q, i, dst, dst, along_x(0, below)).wait_recv()

    class Lane:
        def __init__(self, t, q, which):
            self.t, self.q, self.which = t, q, which
            if which == 0:
                self.m, self.big = x, z
                self.small_dev, self.big_dev = along_x, along_z
                self.g, self.p = ga.at[q], pa.at[q]
            else:
                self.m, self.big = z, x
                self.small_dev, self.big_dev = along_z, along_x
                self.g, self.p = gb.at[q], pb.at[q]
            self.base = which * LANE_COPIES

        def single(self, ref, big, m):
            return ref.at[big, m] if self.which == 0 else ref.at[m, big]

        def group(self, ref, big):
            return ref.at[big] if self.which == 0 else ref.at[:, big]

        def pair(self, ref, big, part):
            two = pl.ds(2 * part, 2)
            return ref.at[big, two] if self.which == 0 else ref.at[two, big]

        def send(self, i, src, dst, dev):
            send(self.q, self.base + i, src, dst, dev)

        def arrived(self, i, dst):
            arrived(self.q, self.base + i, dst)

        def a0(self):
            own = self.single(self.g, self.big, self.m)
            for i, by in enumerate(STEPS):
                self.send(i, own, own, self.small_dev(by))

        def a2(self):
            for i, by in enumerate(STEPS):
                self.arrived(i, self.single(self.g, self.big, wrap(self.m, -by)))
            if RELAY_GATHER:
                one, two = self.pair(self.g, self.big, 0), self.pair(self.g, self.big, 1)
                self.send(3, one, one, self.big_dev(1))
                self.send(4, two, two, self.big_dev(-1))
                self.send(5, two, two, self.big_dev(1))
                self.send(6, one, one, self.big_dev(-1))
            else:
                mine = self.group(self.g, self.big)
                for i, by in enumerate(STEPS):
                    self.send(3 + i, mine, mine, self.big_dev(by))

        def a3(self):
            if RELAY_GATHER:
                one = self.pair(self.g, wrap(self.big, -1), 0)
                two = self.pair(self.g, wrap(self.big, 1), 1)
                self.arrived(3, one)
                self.send(7, one, one, self.big_dev(1))
                self.arrived(4, two)
                self.send(8, two, two, self.big_dev(-1))

        def a4(self):
            if RELAY_GATHER:
                self.arrived(5, self.pair(self.g, wrap(self.big, -1), 1))
                self.arrived(6, self.pair(self.g, wrap(self.big, 1), 0))
                self.arrived(7, self.pair(self.g, wrap(self.big, 2), 0))
                self.arrived(8, self.pair(self.g, wrap(self.big, 2), 1))
            else:
                for i, by in enumerate(STEPS):
                    self.arrived(3 + i, self.group(self.g, wrap(self.big, -by)))

        def slot(self, kind, i):
            return big_p.at[self.q, self.which, 2 * kind + i]

        def r0(self):
            if RELAY_SUM:
                up, down, far = wrap(self.big, 1), wrap(self.big, -1), wrap(self.big, 2)
                self.send(9, self.pair(self.p, far, 0), self.slot(0, 0), self.big_dev(1))
                self.send(10, self.pair(self.p, far, 1), self.slot(0, 1), self.big_dev(-1))
                self.send(11, self.pair(self.p, up, 1), self.slot(1, 0), self.big_dev(1))
                self.send(12, self.pair(self.p, down, 0), self.slot(1, 1), self.big_dev(-1))
            else:
                for i, by in enumerate(STEPS):
                    self.send(
                        9 + i, self.group(self.p, wrap(self.big, by)),
                        big_r.at[self.q, self.which, i], self.big_dev(by),
                    )

        def r1(self):
            if RELAY_SUM:
                for i, by in ((0, 1), (1, -1)):
                    came, both = self.slot(0, i), self.slot(3, i)
                    self.arrived(9 + i, came)
                    own = self.pair(self.p, wrap(self.big, by), i)[...]
                    both[...] = (own.astype(F32) + came[...].astype(F32)).astype(BF)
                    self.send(13 + i, both, self.slot(2, i), self.big_dev(by))

        def r2(self):
            last = self.t == ticks - 1
            total = summed_b.at[self.q, self.which]
            keep = summed.at[self.q % CHUNKS, self.which]
            if RELAY_SUM:
                for i in (0, 1):
                    self.arrived(11 + i, self.slot(1, i))
                    self.arrived(13 + i, self.slot(2, i))
                for part in (0, 1):
                    value = (
                        self.pair(self.p, self.big, part)[...].astype(F32)
                        + self.slot(2, part)[...].astype(F32)
                        + self.slot(1, 1 - part)[...].astype(F32)
                    )
                    if last:
                        keep[pl.ds(2 * part, 2)] = value
                    total[pl.ds(2 * part, 2)] = value.astype(BF)
            else:
                value = self.group(self.p, self.big)[...].astype(F32)
                for i in range(3):
                    self.arrived(9 + i, big_r.at[self.q, self.which, i])
                    value = value + big_r[self.q, self.which, i].astype(F32)
                if last:
                    keep[...] = value
                total[...] = value.astype(BF)
            for i, by in enumerate(STEPS if last else STEPS + (0,)):
                self.send(
                    15 + i, total.at[wrap(self.m, by)],
                    small_r.at[self.q, self.which, i], self.small_dev(by, sec if last else below),
                )

        def total(self):
            last = self.t == ticks - 1
            count = 3 if last else 4
            for i in range(count):
                self.arrived(15 + i, small_r.at[self.q, self.which, i])
            parts = [small_r[self.q, self.which, i].astype(F32) for i in range(count)]
            if last:
                parts.append(summed[self.q % CHUNKS, self.which, self.m])
            return (parts[0] + parts[1]) + (parts[2] + parts[3])

    def normalized(first):
        scale_row = lax.rsqrt(jnp.mean(first * first, axis=-1, keepdims=True) + 1e-06)
        return first * scale_row, scale_row

    def grad_of(first, grad_first, back_lift, gain_row):
        normed, scale_row = normalized(first)
        back_norm = back_lift * gain_row
        back = back_norm - normed * jnp.mean(back_norm * normed, axis=-1, keepdims=True)
        return grad_first + scale_row * back

    class Chunk:
        def __init__(self, t, c, before):
            self.t, self.c, self.q, self.before = t, c, t * CHUNKS + c, before
            self.rows = pl.ds(c * r, r)
            self.lanes = (Lane(t, self.q, 0), Lane(t, self.q, 1))

        def prepare(self, which):
            t, q = self.t, self.q
            mine = held.at[q]
            two = pl.ds(2 * which, 2)
            if t == 0:
                mine[two] = (ct if which else st)[:, self.rows]
            else:
                last_q = self.before.q
                came = got.at[last_q]
                arrived(last_q, PASS + which, came.at[two])
                total = self.before.lanes[which].total()
                if which == 0:
                    values = (came[1] - total, came[0])
                else:
                    values = (came[3], grad_of(came[0], came[2], total, gain_above[...]))
                feed = fc if which else fs
                for i in (0, 1):
                    mine[2 * which + i] = jnp.where(top, feed[t - 1, i, self.rows], values[i])
            if which == 0:
                ga[q, z, x] = (normalized(mine[0])[0] * gain[...]).astype(BF)
            else:
                gb[q, z, x] = mine[3].astype(BF)

        def start(self, which):
            t, q = self.t, self.q
            two = pl.ds(2 * which, 2)
            if t > 0:
                self.prepare(which)
            self.lanes[which].a0()
            if t < ticks - 1:
                send(q, PASS + which, held.at[q, two], got.at[q, two], along_x(0, below))

        def finish(self, which):
            mine = held.at[self.q]
            total = self.lanes[which].total()
            if which == 0:
                out_s[0, 0, self.rows], out_s[0, 1, self.rows] = mine[1] - total, mine[0]
            else:
                out_c[0, 0, self.rows] = mine[3]
                out_c[0, 1, self.rows] = grad_of(mine[0], mine[2], total, gain[...])

        def tiles(self, body, size):
            def step(j, carry):
                body(pl.ds(pl.multiple_of(j * TILE, TILE), TILE))
                return carry

            lax.fori_loop(0, size // TILE, step, 0)

        def k1(self, which):
            q, c = self.q, self.c

            def lifted(cols):
                pre = dot_nn(ga[q].reshape(n, width), w_in[:, cols])
                sq = pre * pre
                th = jnp.tanh(pre * (GELU_C + (GELU_C * GELU_A) * sq))
                cdf = 0.5 + 0.5 * th
                hid[q, :, cols] = (pre * cdf).astype(BF)
                slope[c, :, cols] = cdf + (0.5 * pre) * (1.0 - th * th) * (
                    GELU_C + (3.0 * GELU_C * GELU_A) * sq
                )

            def cotan(cols):
                back = dot_nt(gb[q].reshape(n, width), w_out[cols, :])
                bpre[q, :, cols] = (back * slope[c, :, cols]).astype(BF)

            self.tiles(cotan if which else lifted, w_in.shape[1])

        def k2(self, which):
            q = self.q

            def block_out(cols):
                out = dot_nn(hid[q], w_out[:, cols])
                pa[q, :, :, :, cols] = out.astype(BF).reshape(SIDE, SIDE, r, TILE)

            def back_lift(cols):
                out = dot_nt(bpre[q], w_in[cols, :])
                pb[q, :, :, :, cols] = out.astype(BF).reshape(SIDE, SIDE, r, TILE)

            self.tiles(back_lift if which else block_out, width)

    def weight_piece(t, which, lo, count):
        left, right, acc = (ga, bpre, out_gin) if which == 0 else (hid, gb, out_gout)

        def whole(ref, cols):
            if ref is ga or ref is gb:
                parts = [ref[t * CHUNKS + c, :, :, :, cols].reshape(n, -1) for c in range(CHUNKS)]
            else:
                parts = [ref[t * CHUNKS + c, :, cols] for c in range(CHUNKS)]
            return jnp.concatenate(parts, axis=0)

        def body(j, carry):
            cols = pl.ds(pl.multiple_of(j * GRAD_TILE, GRAD_TILE), GRAD_TILE)
            part = dot_tn(whole(left, cols), whole(right, pl.ds(0, width)))
            acc[0, cols, :] = part if t == 0 else acc[0, cols, :] + part
            return carry

        first = lo * 256 // GRAD_TILE
        lax.fori_loop(first, first + count * 256 // GRAD_TILE, body, 0)

    chunks = {}
    for t in range(ticks):
        for c in range(CHUNKS):
            chunks[t, c] = Chunk(t, c, chunks.get((t - 1, c)))
    pending = {}

    def once(key, run):
        if key not in pending:
            pending[key] = True
            run()

    def wait_all(copies):
        for copy in copies:
            copy.wait()

    for c in range(CHUNKS):
        for which in (0, 1):
            chunks[0, c].prepare(which)
    pl.semaphore_wait(barrier, len(peers))
    later = []

    def load_rest():
        later.extend([load(3, w_in_hbm.at[0], w_in), load(4, w_out_hbm.at[0], w_out)])
        later.extend([load(5, feed_s, fs), load(6, feed_c, fc)])

    for t, c, which, what in order(ticks):
        if what != "S":
            once("rest", load_rest)
        if what == "W":
            weight_piece(t, c, which, 2)
            continue
        chunk = chunks[t, c]
        if what == "S":
            if t > 0:
                once("feed", lambda: wait_all(later[2:]))
                if which == 1:
                    once("gain", lambda: arrived(0, PASS + 2, gain_above))
            chunk.start(which)
            once("gain_sent", lambda: send(0, PASS + 2, gain, gain_above, along_x(0, below)))
        elif what == "F":
            chunk.finish(which)
        elif what == "K1":
            once("weights", lambda: wait_all(later[:2]))
            chunk.k1(which)
        elif what == "K2":
            chunk.k2(which)
        else:
            getattr(chunk.lanes[which], what)()
    for sent_q, i, src in waits:
        remote(sent_q, i, src, src, along_x(0, below)).wait_send()


def shards(streams, cotangents, feed_streams, feed_cotangents, w_in, w_out, gain):
    ticks = feed_streams.shape[0] + 1
    rows, width = streams.shape[2], streams.shape[3]
    hidden = w_in.shape[2]
    r = rows // CHUNKS
    n = SIDE * SIDE * r
    q = ticks * CHUNKS
    blocks = (q, SIDE, SIDE, r, width)
    hbm = pl.BlockSpec(memory_space=pltpu.HBM)
    vmem = pl.BlockSpec(memory_space=pltpu.VMEM)
    outs = (streams.shape, cotangents.shape, w_in.shape, w_out.shape)
    held_outs = pl.pallas_call(
        kernel,
        out_shape=tuple(pltpu.VMEM(s, F32) for s in outs),
        in_specs=[hbm] * 7,
        out_specs=(vmem,) * 4,
        scratch_shapes=[
            pltpu.VMEM((2, rows, width), F32),
            pltpu.VMEM((2, rows, width), F32),
            pltpu.VMEM(feed_streams.shape, F32),
            pltpu.VMEM(feed_cotangents.shape, F32),
            pltpu.VMEM((width, hidden), BF),
            pltpu.VMEM((hidden, width), BF),
            pltpu.VMEM((1, width), F32),
            pltpu.VMEM((1, width), F32),
            pltpu.VMEM((q, 4, r, width), F32),
            pltpu.VMEM((q - CHUNKS, 4, r, width), F32),
            pltpu.VMEM(blocks, BF),
            pltpu.VMEM(blocks, BF),
            pltpu.VMEM((q, n, hidden), BF),
            pltpu.VMEM((q, n, hidden), BF),
            pltpu.VMEM(blocks, BF),
            pltpu.VMEM(blocks, BF),
            pltpu.VMEM((q, 2, 8, 2, r, width), BF),
            pltpu.VMEM((CHUNKS, n, hidden), F32),
            pltpu.VMEM((CHUNKS, 2, SIDE, r, width), F32),
            pltpu.VMEM((q, 2, SIDE, r, width), BF),
            pltpu.VMEM((q, 2, 4, r, width), BF),
            pltpu.SemaphoreType.DMA((q, N_COPY)),
            pltpu.SemaphoreType.DMA((q, N_COPY)),
            pltpu.SemaphoreType.DMA((8,)),
        ],
        compiler_params=pltpu.CompilerParams(
            collective_id=0, has_side_effects=True, vmem_limit_bytes=50 * 1024 * 1024
        ),
    )(streams, cotangents, feed_streams, feed_cotangents, w_in, w_out, gain)
    parts = [(2, k) for k in range(8)] + [(3, k) for k in range(8)] + [(0, 0), (1, 0)]

    def store(*refs):
        outs_in, outs_to, sems = refs[:4], refs[4:8], refs[8]
        copies = []
        for i, (which, k) in enumerate(parts):
            src, dst = outs_in[which].at[0], outs_to[which].at[0]
            if which >= 2:
                span = pl.ds(k * (src.shape[0] // 8), src.shape[0] // 8)
                src, dst = src.at[span], dst.at[span]
            copies.append(pltpu.make_async_copy(src, dst, sems.at[i]))
            copies[-1].start()
        for copy in copies:
            copy.wait()

    return pl.pallas_call(
        store,
        out_shape=tuple(jax.ShapeDtypeStruct(s, F32) for s in outs),
        in_specs=[vmem] * 4,
        out_specs=(hbm,) * 4,
        scratch_shapes=[pltpu.SemaphoreType.DMA((len(parts),))],
        compiler_params=pltpu.CompilerParams(vmem_limit_bytes=4 * 1024 * 1024),
    )(*[pltpu.with_memory_space_constraint(a, pltpu.VMEM) for a in held_outs])


def solution(mesh):
    placed = (
        P("section", None, "hid", None),
        P("section", None, "hid", None),
        P(None, None, "hid", None),
        P(None, None, "hid", None),
        P("section", None, "hid"),
        P("section", "hid", None),
        P("section", None),
    )
    return jax.shard_map(
        shards,
        mesh=mesh,
        in_specs=placed,
        out_specs=(
            P("section", None, "hid", None),
            P("section", None, "hid", None),
            P("section", None, "hid"),
            P("section", "hid", None),
        ),
        check_vma=False,
    )
```
